256 devices in a mesh: clus: 32 (over y, z), samp: 8 (over x, core).
Axes of the slice: x: 4, y: 4, z: 8, core: 2. Of those that a mesh axis runs over, the one named last changes fastest.
Arguments:
- currents: float32 [2048, 2, 128], P(('clus', 'samp')), may hold values from -6 to 6
- near_blocks: float32 [2048, 8, 2, 128, 128], P(('clus', 'samp')), may hold values from -0.125 to 0.125
- neighbours: int32 [2048, 8], P(('clus', 'samp')), may hold values from 0 to 2047, as said below
- near_count: int32 [2048], P(('clus', 'samp')), may hold values from 4 to 8
- radiation: float32 [2048, 2, 2, 128, 128], P(('clus', 'samp')), may hold values from -0.375 to 0.375
- interp_leaf: float32 [128, 256], replicated, may hold values from -0.1875 to 0.1875
- phase_leaf: float32 [8, 256], replicated, may hold values from -3.140625 to 3.140625
- interp_upper: float32 [256, 768], P(None, 'samp'), may hold values from -0.125 to 0.125
- phase_upper: float32 [8, 768], P(None, 'samp'), may hold values from -3.140625 to 3.140625
- tables_lower: float32 [64, 2, 256], replicated, may hold values from -1 to 1
- operator_lower: int32 [256, 16], replicated, may hold values from 0 to 63
- sources_lower: int32 [256, 16], replicated, may hold values from 0 to 255, as said below
- count_lower: int32 [256], replicated, may hold values from 8 to 16
- tables_upper: float32 [64, 2, 768], P(None, None, 'samp'), may hold values from -1.5 to 1.5
- operator_upper: int32 [32, 7], replicated, may hold values from 0 to 63
- sources_upper: int32 [32, 7], replicated, may hold values from 0 to 31, as said below
- count_upper: int32 [32], replicated, may hold values from 3 to 7
Outputs:
- near_field: float32 [2048, 2, 128], P(('clus', 'samp'))
- incoming_lower: float32 [256, 2, 2, 256], P(('clus', 'samp'))
- incoming_upper: float32 [32, 2, 2, 768], P('clus', None, None, 'samp')
The draws below stay inside these ranges and needn't reach their ends.
Inputs may be any that keep to these rules, and one draw needn't show every extreme that they name: `neighbours`: the first slot of each leaf box is the box itself; every entry lies within 8 of its row's box index. `sources_lower`: the entries of a row are distinct and differ from the row's own box. `sources_upper`: the entries of a row are distinct and differ from the row's own box.
All inputs are finite; a program needn't handle non-finite values.
Results may differ from the reference program's by a relative error of at most 0.00007.
Values sent between devices are 32-bit elements; how exact they have to be, the bound alone decides.
No kernel may reach another device: no remote copies, remote signals or barrier semaphores. Data moves between devices by JAX's collectives and lax.ppermute only.
A program may use at most 64 MiB of HBM per device.

```python
import jax
import jax.numpy as jnp
from jax import lax

M = 128
NBR = 8
K0 = 128
K1 = 256
K2 = 768
NI1 = 16
NI2 = 7
NT = 64
BOX_DEV = 8
BOXES = 2048
BOX1 = 256
BOX2 = 32


def listed_sources(key, box_total, slot_count):
    row_keys = jax.random.split(key, box_total)

    def shuffled(single_key):
        return jax.random.permutation(single_key, box_total - 1)[:slot_count]
    offsets = jax.vmap(shuffled)(row_keys) + 1
    box_index = jnp.arange(box_total)[:, None]
    return ((box_index + offsets) % box_total).astype(jnp.int32)


def draw_neighbours(key, part):
    offsets = jax.random.randint(key, (BOXES, NBR), -BOX_DEV, BOX_DEV + 1)
    slot_index = jnp.arange(NBR)[None, :]
    offsets = jnp.where(slot_index == 0, 0, offsets)
    box_index = jnp.arange(BOXES)[:, None]
    return jnp.clip(box_index + offsets, 0, BOXES - 1).astype(jnp.int32)


def draw_sources_lower(key, part):
    return listed_sources(jax.random.fold_in(key, 11), BOX1, NI1)


def draw_sources_upper(key, part):
    return listed_sources(jax.random.fold_in(key, 23), BOX2, NI2)


def set_ends(array, own_key, smallest, top_value):
    longest = array.shape.index(max(array.shape))
    spots = []
    for shift in (0, 1):
        where = [jax.random.randint(jax.random.fold_in(own_key, axis), (), 0, length) for axis, length in enumerate(array.shape)]
        where[longest] = (where[longest] + shift) % array.shape[longest]
        spots.append(tuple(where))
    return array.at[spots[0]].set(smallest).at[spots[1]].set(top_value)


def block_scale(own_key, shape, pieces, low, top_value):
    level = 1.0
    for axis_at, blocks in pieces:
        heights = jax.random.uniform(jax.random.fold_in(jax.random.fold_in(own_key, 6), axis_at), (blocks,), jnp.float32, low / len(pieces), top_value / len(pieces))
        level = level * jnp.repeat(jnp.exp(heights), shape[axis_at] // blocks).reshape((-1,) + (1,) * (len(shape) - 1 - axis_at))
    return level


def normal_values(rng, shape, spread, most, shards=(), dtype=jnp.bfloat16):
    entries = jax.random.normal(rng, shape, jnp.float32) * spread
    if len(shards) > 0:
        entries = block_scale(rng, shape, shards, -0.22, 0.18) * entries
    return jnp.clip(entries, min=-most, max=most).astype(dtype)


def setup_inputs(seed: int = 0) -> dict:
    keys = jax.random.split(jax.random.key(seed), 18)
    currents = normal_values(keys[0], (BOXES, 2, M), 1.0, 6.0, ((0, 256),), jnp.float32)
    near_blocks = normal_values(keys[1], (BOXES, NBR, 2, M, M), (2 * NBR * M) ** -0.5, 0.125, ((0, 256),), jnp.float32)
    neighbours = draw_neighbours(jax.random.fold_in(keys[17], 71), 0)
    near_count = set_ends(jax.random.randint(keys[3], (BOXES,), NBR // 2, NBR + 1), jax.random.fold_in(keys[3], 1), NBR // 2, NBR).astype(jnp.int32)
    radiation = normal_values(keys[4], (BOXES, 2, 2, M, K0), (2 * M) ** -0.5, 0.375, ((0, 256),), jnp.float32)
    interp_leaf = normal_values(keys[5], (K0, K1), (8 * K0) ** -0.5, 0.1875, (), jnp.float32)
    phase_leaf = jnp.clip(jax.random.uniform(keys[6], (8, K1), jnp.float32, -3.140625, 3.140625), -3.140625, 3.140625)
    interp_upper = normal_values(keys[7], (K1, K2), (8 * K1) ** -0.5, 0.125, ((1, 8),), jnp.float32)
    phase_upper = jnp.clip(jax.random.uniform(keys[8], (8, K2), jnp.float32, -3.140625, 3.140625), -3.140625, 3.140625)
    tables_lower = normal_values(keys[9], (NT, 2, K1), (2 * NI1) ** -0.5, 1.0, (), jnp.float32)
    operator_lower = set_ends(jax.random.randint(keys[10], (BOX1, NI1), 0, NT), jax.random.fold_in(keys[10], 1), 0, NT - 1).astype(jnp.int32)
    sources_lower = draw_sources_lower(jax.random.fold_in(keys[17], 71), 0)
    count_lower = set_ends(jax.random.randint(keys[12], (BOX1,), NI1 // 2, NI1 + 1), jax.random.fold_in(keys[12], 1), NI1 // 2, NI1).astype(jnp.int32)
    tables_upper = normal_values(keys[13], (NT, 2, K2), (2 * NI2) ** -0.5, 1.5, ((2, 8),), jnp.float32)
    operator_upper = set_ends(jax.random.randint(keys[14], (BOX2, NI2), 0, NT), jax.random.fold_in(keys[14], 1), 0, NT - 1).astype(jnp.int32)
    sources_upper = draw_sources_upper(jax.random.fold_in(keys[17], 71), 0)
    count_upper = set_ends(jax.random.randint(keys[16], (BOX2,), NI2 // 2, NI2 + 1), jax.random.fold_in(keys[16], 1), NI2 // 2, NI2).astype(jnp.int32)
    return {"currents": currents, "near_blocks": near_blocks, "neighbours": neighbours, "near_count": near_count, "radiation": radiation, "interp_leaf": interp_leaf, "phase_leaf": phase_leaf, "interp_upper": interp_upper, "phase_upper": phase_upper, "tables_lower": tables_lower, "operator_lower": operator_lower, "sources_lower": sources_lower, "count_lower": count_lower, "tables_upper": tables_upper, "operator_upper": operator_upper, "sources_upper": sources_upper, "count_upper": count_upper}


highest = lax.Precision.HIGHEST


def shift_children(values, phases):
    cosine = jnp.cos(phases)[None, :, None, :]
    sine_part = jnp.sin(phases)[None, :, None, :]
    real_part = values[:, :, :, 0]
    imag_part = values[:, :, :, 1]
    moved = jnp.stack([cosine * real_part - sine_part * imag_part, sine_part * real_part + cosine * imag_part], axis=3)
    return jnp.sum(moved, axis=1)


def translate_listed(patterns, sources, operators, counts, columns):
    picked = patterns[sources]
    weights = columns[operators]
    slot_count = sources.shape[1]
    usable = (jnp.arange(slot_count)[None, :] < counts[:, None]).astype(jnp.float32)
    weights = weights * usable[:, :, None, None]
    w_real = weights[:, :, None, 0]
    w_imag = weights[:, :, None, 1]
    p_real = picked[:, :, :, 0]
    p_imag = picked[:, :, :, 1]
    out_real = jnp.sum(w_real * p_real - w_imag * p_imag, axis=1)
    out_imag = jnp.sum(w_real * p_imag + w_imag * p_real, axis=1)
    return jnp.stack([out_real, out_imag], axis=2)


def near_group(operands):
    block_group, fetched_group = operands
    products = jnp.einsum("bkcij,bkdj->bcdi", block_group, fetched_group, precision=highest)
    return jnp.stack([products[:, 0, 0] - products[:, 1, 1], products[:, 0, 1] + products[:, 1, 0]], axis=1)


def reference(currents, near_blocks, neighbours, near_count, radiation, interp_leaf, phase_leaf, interp_upper, phase_upper, tables_lower, operator_lower, sources_lower, count_lower, tables_upper, operator_upper, sources_upper, count_upper):
    fetched = currents[neighbours]
    usable = (jnp.arange(NBR)[None, :] < near_count[:, None]).astype(jnp.float32)
    fetched = fetched * usable[:, :, None, None]
    grouped = lax.map(near_group, (near_blocks.reshape(BOXES // 8, 8, NBR, 2, M, M), fetched.reshape(BOXES // 8, 8, NBR, 2, M)))
    near_field = grouped.reshape(BOXES, 2, M)
    radiated = jnp.einsum("bpcmk,bdm->bpcdk", radiation, currents, precision=highest)
    leaf_patterns = jnp.stack([radiated[:, :, 0, 0] - radiated[:, :, 1, 1], radiated[:, :, 0, 1] + radiated[:, :, 1, 0]], axis=2)
    interpolated = jnp.einsum("bpck,kt->bpct", leaf_patterns, interp_leaf, precision=highest)
    lower_patterns = shift_children(interpolated.reshape(BOX1, 8, 2, 2, K1), phase_leaf)
    incoming_lower = translate_listed(lower_patterns, sources_lower, operator_lower, count_lower, tables_lower)
    lifted = jnp.einsum("qpct,tu->qpcu", lower_patterns, interp_upper, precision=highest)
    upper_patterns = shift_children(lifted.reshape(BOX2, 8, 2, 2, K2), phase_upper)
    incoming_upper = translate_listed(upper_patterns, sources_upper, operator_upper, count_upper, tables_upper)
    return near_field, incoming_lower, incoming_upper
```

```python
import functools

import jax
import jax.numpy as jnp
from jax import lax
from jax.experimental import pallas as pl
from jax.experimental.pallas import tpu as pltpu
from jax.sharding import Mesh
from jax.sharding import PartitionSpec as P

CLUS = ("clus_0", "clus_1")
SAMP = ("samp_0", "samp_1")
CLUS_SAMP = CLUS + SAMP

HIGHEST = lax.Precision.HIGHEST
F32 = jnp.float32
VMEM = pl.BlockSpec(memory_space=pltpu.VMEM)
SMEM = pl.BlockSpec(memory_space=pltpu.SMEM)
HBM = pl.BlockSpec(memory_space=pltpu.HBM)


def place():
    clus = lax.axis_index("clus_0") * 8 + lax.axis_index("clus_1")
    samp = lax.axis_index("samp_0") * 2 + lax.axis_index("samp_1")
    return clus, samp


def call(kernel, outs, in_specs, scratch=(), mib=16, flops=0, bytes_accessed=0, name=None):
    many = isinstance(outs, (list, tuple))
    run = pl.pallas_call(
        kernel,
        out_shape=outs,
        in_specs=in_specs,
        out_specs=[VMEM] * len(outs) if many else VMEM,
        scratch_shapes=list(scratch),
        compiler_params=pltpu.CompilerParams(vmem_limit_bytes=mib << 20),
        cost_estimate=pl.CostEstimate(flops=flops, bytes_accessed=bytes_accessed, transcendentals=0),
        name=name,
    )

    def placed(*operands):
        return run(
            *(
                pltpu.with_memory_space_constraint(x, pltpu.HBM) if spec is HBM else x
                for x, spec in zip(operands, in_specs)
            )
        )

    return placed


def rows_of(shape, axis):
    return lax.broadcasted_iota(jnp.int32, shape, axis)


def start_all(pairs, sems):
    copies = [pltpu.make_async_copy(a, b, sems.at[i]) for i, (a, b) in enumerate(pairs)]
    for copy in copies:
        copy.start()
    return copies


def leaf_kernel(cur_h, rad_h, interp_h, phase_h, out, cur, rad, interp, phase, pat, msg, sems):
    pairs = [(cur_h, cur)] + [(rad_h.at[b], rad.at[b]) for b in range(8)] + [(interp_h, interp), (phase_h, phase)]
    copies = start_all(pairs, sems)
    copies[0].wait()
    columns = cur[...].reshape(16, 128).T
    for b in range(8):
        copies[1 + b].wait()
        cr = jnp.broadcast_to(columns[:, 2 * b : 2 * b + 1], (128, 128))
        ci = jnp.broadcast_to(columns[:, 2 * b + 1 : 2 * b + 2], (128, 128))
        for p in range(2):
            rr = rad[b, p, 0]
            ri = rad[b, p, 1]
            pat[pl.ds(16 * p + b, 1), :] = jnp.sum(rr * cr - ri * ci, axis=0, keepdims=True)
            pat[pl.ds(16 * p + 8 + b, 1), :] = jnp.sum(rr * ci + ri * cr, axis=0, keepdims=True)
    copies[9].wait()
    copies[10].wait()
    lifted = jnp.dot(pat[...], interp[...], precision=HIGHEST, preferred_element_type=F32)
    cosine = jnp.cos(phase[...])
    sine = jnp.sin(phase[...])
    for p in range(2):
        yr = lifted[16 * p : 16 * p + 8]
        yi = lifted[16 * p + 8 : 16 * p + 16]
        re = jnp.sum(cosine * yr - sine * yi, axis=0, keepdims=True)
        im = jnp.sum(sine * yr + cosine * yi, axis=0, keepdims=True)
        for c, part in enumerate((re, im)):
            for h in range(2):
                msg[pl.ds(4 * p + 2 * c + h, 1), :] = part[:, 128 * h : 128 * h + 128]
    whole = msg[...]
    for peer in range(8):
        out[peer] = whole


def prep_kernel(
    src_low_h, op_low_h, cnt_low_h, src_up_h, op_up_h, cnt_up_h, tab_low_h, tab_up_h, phase_h, interp_h,
    wa, wb, ua, ub, rot, interp,
    src_low, op_low, cnt_low, src_up, op_up, cnt_up, tab_low, tab_up, phase, code_v, code_s, sem, sems,
):
    clus, samp = place()
    copies = start_all(
        [
            (src_low_h, src_low), (op_low_h, op_low), (cnt_low_h, cnt_low), (src_up_h, src_up),
            (op_up_h, op_up), (cnt_up_h, cnt_up), (phase_h, phase), (tab_low_h, tab_low),
            (tab_up_h, tab_up), (interp_h, interp),
        ],
        sems,
    )
    for copy in copies:
        copy.wait()
    src = src_low[...]
    used = (rows_of(src.shape, 0) < cnt_low[...]) & ((src >> 3) == clus)
    code = op_low[...] + 1
    octant = src & 7
    for o in range(8):
        code_v[pl.ds(o, 1), :] = jnp.sum(jnp.where(used & (octant == o), code, 0), axis=0, keepdims=True)
    code_v[pl.ds(8, 8), :] = jnp.zeros((8, 256), jnp.int32)
    used_up = (rows_of(src_up.shape, 0) < cnt_up[...]) & (src_up[...] == clus)
    code_v[pl.ds(8, 1), pl.ds(0, 32)] = jnp.sum(jnp.where(used_up, op_up[...] + 1, 0), axis=0, keepdims=True)
    copy = pltpu.make_async_copy(code_v, code_s, sem)
    copy.start()
    zero = jnp.zeros((8, 128), F32)
    row = rows_of((8, 128), 0)
    first_half = (row & 1) == 0
    sign_low = jnp.where((row & 2) == 0, -1.0, 1.0).astype(F32)
    sign_up = jnp.where((row & 1) == 0, -1.0, 1.0).astype(F32)[:, :96]
    rot[0] = zero
    rot[1] = zero
    rot[0, :, pl.ds(0, 96)] = jnp.cos(phase[...])
    rot[1, :, pl.ds(0, 96)] = jnp.sin(phase[...])
    copy.wait()

    def target(t, carry):
        for o in range(8):
            i = code_s[o, t * 8 + samp]
            n = jnp.maximum(i - 1, 0)
            listed = jnp.where(i > 0, 1.0, 0.0).astype(F32)
            parts = []
            for c in range(2):
                low = jnp.broadcast_to(tab_low[n, pl.ds(c, 1), pl.ds(0, 128)], (8, 128))
                high = jnp.broadcast_to(tab_low[n, pl.ds(c, 1), pl.ds(128, 128)], (8, 128))
                parts.append(jnp.where(first_half, low, high) * listed)
            wa[t, o] = parts[0]
            wb[t, o] = parts[1] * sign_low
        i = code_s[8, t]
        n = jnp.maximum(i - 1, 0)
        listed = jnp.where(i > 0, 1.0, 0.0).astype(F32)
        ua[t] = zero
        ub[t] = zero
        ua[t, :, pl.ds(0, 96)] = jnp.broadcast_to(tab_up[n, pl.ds(0, 1), :], (8, 96)) * listed
        ub[t, :, pl.ds(0, 96)] = jnp.broadcast_to(tab_up[n, pl.ds(1, 1), :], (8, 96)) * listed * sign_up
        return carry

    lax.fori_loop(0, 32, target, 0)


def middle_kernel(got, interp, wa, wb, ua, ub, rot, out, upper):
    row = rows_of((8, 128), 0)
    halves = []
    for h in range(2):
        halves.append(
            jnp.concatenate([got[pl.ds(2 * k + h, 8, stride=8), :] for k in range(4)], axis=0)
        )
    lifted = lax.dot_general(
        jnp.concatenate(halves, axis=1), interp[...], (((1,), (1,)), ((), ())),
        precision=HIGHEST, preferred_element_type=F32,
    )
    plain = [got[pl.ds(8 * o, 8), :] for o in range(8)]
    swapped = [
        jnp.where((row & 2) == 0, pltpu.roll(x, 6, 0), pltpu.roll(x, 2, 0)) for x in plain
    ]
    for t in range(32):
        total = wa[t, 0] * plain[0] + wb[t, 0] * swapped[0]
        for o in range(1, 8):
            total += wa[t, o] * plain[o] + wb[t, o] * swapped[o]
        out[t, pl.ds(0, 8), :] = total
    upper[...] = jnp.zeros((8, 128), F32)
    cosine = rot[0][:, :96]
    sine = rot[1][:, :96]
    for p in range(2):
        zr = lifted[16 * p : 16 * p + 8]
        zi = lifted[16 * p + 8 : 16 * p + 16]
        upper[pl.ds(2 * p, 1), pl.ds(0, 96)] = jnp.sum(cosine * zr - sine * zi, axis=0, keepdims=True)
        upper[pl.ds(2 * p + 1, 1), pl.ds(0, 96)] = jnp.sum(sine * zr + cosine * zi, axis=0, keepdims=True)
    up = upper[...]
    up_swapped = jnp.where((row & 1) == 0, pltpu.roll(up, 7, 0), pltpu.roll(up, 1, 0))
    for t in range(32):
        out[t, pl.ds(8, 8), :] = ua[t] * up + ub[t] * up_swapped


def near_kernel(cur, low, high, neighbours_h, count_h, blocks, out, held, ext, acc, neighbours, count, sems):
    clus, samp = place()
    base = (clus * 8 + samp) * 8 - 8

    def copy(b):
        return pltpu.make_async_copy(blocks.at[b], held.at[b], sems.at[b])

    for b in range(8):
        copy(b).start()
    lists = [
        pltpu.make_async_copy(cur, ext.at[pl.ds(8, 8)], sems.at[8]),
        pltpu.make_async_copy(neighbours_h, neighbours, sems.at[9]),
        pltpu.make_async_copy(count_h, count, sems.at[10]),
    ]
    for one in lists:
        one.start()
    ext[pl.ds(0, 8)] = low[...]
    ext[pl.ds(16, 8)] = high[...]
    for one in lists:
        one.wait()
    ones = jnp.ones((8, 128), F32)

    def box(b, carry):
        xs = []
        for k in range(8):
            i = neighbours[b, k] - base
            keep = jnp.where(k < count[b], 1.0, 0.0).astype(F32)
            xr = jnp.broadcast_to(ext[i, pl.ds(0, 1), :], (8, 128)) * keep
            xi = jnp.broadcast_to(ext[i, pl.ds(1, 1), :], (8, 128)) * keep
            xs.append((xr, xi))
        copy(b).wait()
        for it in range(16):
            re = None
            for k, (xr, xi) in enumerate(xs):
                br = held[b, k, 0, pl.ds(8 * it, 8), :]
                bi = held[b, k, 1, pl.ds(8 * it, 8), :]
                tr = br * xr - bi * xi
                ti = br * xi + bi * xr
                re, im = (tr, ti) if re is None else (re + tr, im + ti)
            acc[0, pl.ds(8 * it, 8), :] = re
            acc[1, pl.ds(8 * it, 8), :] = im
        for c in range(2):
            summed = lax.dot_general(
                ones, acc[c], (((1,), (1,)), ((), ())), precision=HIGHEST, preferred_element_type=F32
            )
            out[b, pl.ds(c, 1), :] = summed[0:1]
        return carry

    lax.fori_loop(0, 8, box, 0)


def final_kernel(got, out_low, out_up):
    low = got[0, pl.ds(0, 8), :]
    up = got[0, pl.ds(8, 8), :]
    for t in range(1, 32):
        low += got[t, pl.ds(0, 8), :]
        up += got[t, pl.ds(8, 8), :]
    for p in range(2):
        for c in range(2):
            k = 2 * p + c
            for h in range(2):
                out_low[0, p, pl.ds(c, 1), pl.ds(128 * h, 128)] = low[2 * k + h : 2 * k + h + 1]
            out_up[0, p, pl.ds(c, 1), :] = up[k : k + 1, :96]


def shape(*dims):
    return jax.ShapeDtypeStruct(dims, F32)


def local(
    currents, near_blocks, neighbours, near_count, radiation, interp_leaf, phase_leaf,
    interp_upper, phase_upper, tables_lower, operator_lower, sources_lower, count_lower,
    tables_upper, operator_upper, sources_upper, count_upper,
):
    message = call(
        leaf_kernel, shape(8, 8, 128), [HBM] * 4,
        [
            pltpu.VMEM((8, 2, 128), F32), pltpu.VMEM((8, 2, 2, 128, 128), F32),
            pltpu.VMEM((128, 256), F32), pltpu.VMEM((8, 256), F32),
            pltpu.VMEM((32, 128), F32), pltpu.VMEM((8, 128), F32), pltpu.SemaphoreType.DMA((11,)),
        ],
        flops=4 << 20, bytes_accessed=2 << 20, name="leaf",
    )(currents, radiation, interp_leaf, phase_leaf)
    own, message = lax.optimization_barrier((currents, message))
    gathered = lax.all_to_all(message, SAMP, split_axis=0, concat_axis=0, tiled=True)

    size = lax.axis_size(CLUS_SAMP)
    up = [(i, i + 1) for i in range(size - 1)]
    down = [(b, a) for a, b in up]
    low = lax.ppermute(own, CLUS_SAMP, up)
    high = lax.ppermute(own, CLUS_SAMP, down)

    wa, wb, ua, ub, rot, interp = call(
        prep_kernel,
        [
            shape(32, 8, 8, 128), shape(32, 8, 8, 128), shape(32, 8, 128), shape(32, 8, 128),
            shape(2, 8, 128), shape(96, 256),
        ],
        [HBM] * 10,
        [
            pltpu.VMEM((16, 256), jnp.int32), pltpu.VMEM((16, 256), jnp.int32), pltpu.VMEM((1, 256), jnp.int32),
            pltpu.VMEM((7, 32), jnp.int32), pltpu.VMEM((7, 32), jnp.int32), pltpu.VMEM((1, 32), jnp.int32),
            pltpu.VMEM((64, 2, 256), F32), pltpu.VMEM((64, 2, 96), F32), pltpu.VMEM((8, 96), F32),
            pltpu.VMEM((16, 256), jnp.int32), pltpu.SMEM((16, 256), jnp.int32), pltpu.SemaphoreType.DMA,
            pltpu.SemaphoreType.DMA((10,)),
        ],
        flops=1 << 20, bytes_accessed=4 << 20, name="prep",
    )(
        sources_lower.T, operator_lower.T, count_lower.reshape(1, -1),
        sources_upper.T, operator_upper.T, count_upper.reshape(1, -1),
        tables_lower, tables_upper, phase_upper, interp_upper.T,
    )

    payload = call(
        middle_kernel, shape(32, 16, 128), [VMEM] * 7, [pltpu.VMEM((8, 128), F32)],
        flops=4 << 20, bytes_accessed=3 << 20, name="middle",
    )(gathered.reshape(64, 128), interp, wa, wb, ua, ub, rot)
    parts = lax.all_to_all(payload, CLUS, split_axis=0, concat_axis=0, tiled=True)

    near_field = call(
        near_kernel, shape(8, 2, 128), [HBM, VMEM, VMEM, HBM, HBM, HBM],
        [
            pltpu.VMEM((8, 8, 2, 128, 128), F32),
            pltpu.VMEM((24, 2, 128), F32),
            pltpu.VMEM((2, 128, 128), F32),
            pltpu.SMEM((8, 8), jnp.int32),
            pltpu.SMEM((8,), jnp.int32),
            pltpu.SemaphoreType.DMA((11,)),
        ],
        flops=16 << 20, bytes_accessed=8 << 20, name="near",
    )(currents, low, high, neighbours, near_count, near_blocks)

    incoming_lower, incoming_upper = call(
        final_kernel, [shape(1, 2, 2, 256), shape(1, 2, 2, 96)], [VMEM],
        flops=1 << 17, bytes_accessed=1 << 18, name="final",
    )(parts)
    return near_field, incoming_lower, incoming_upper


def solution(mesh):
    split = Mesh(mesh.devices.reshape(4, 8, 4, 2), CLUS_SAMP)
    whole = P()
    return jax.shard_map(
        local,
        mesh=split,
        in_specs=(
            P(CLUS_SAMP), P(CLUS_SAMP), P(CLUS_SAMP), P(CLUS_SAMP), P(CLUS_SAMP),
            whole, whole, P(None, SAMP), P(None, SAMP),
            whole, whole, whole, whole, P(None, None, SAMP), whole, whole, whole,
        ),
        out_specs=(P(CLUS_SAMP), P(CLUS_SAMP), P(CLUS, None, None, SAMP)),
        check_vma=False,
    )
```

```python
import functools

import jax
import jax.numpy as jnp
from jax import lax
from jax.experimental import pallas as pl
from jax.experimental.pallas import tpu as pltpu
from jax.sharding import Mesh
from jax.sharding import PartitionSpec as P

CLUS = ("clus_0", "clus_1")
SAMP = ("samp_0", "samp_1")
CLUS_SAMP = CLUS + SAMP

HIGHEST = lax.Precision.HIGHEST
F32 = jnp.float32
VMEM = pl.BlockSpec(memory_space=pltpu.VMEM)
SMEM = pl.BlockSpec(memory_space=pltpu.SMEM)
HBM = pl.BlockSpec(memory_space=pltpu.HBM)


def place():
    clus = lax.axis_index("clus_0") * 8 + lax.axis_index("clus_1")
    samp = lax.axis_index("samp_0") * 2 + lax.axis_index("samp_1")
    return clus, samp


def call(kernel, outs, in_specs, scratch=(), mib=16, flops=0, bytes_accessed=0, name=None):
    many = isinstance(outs, (list, tuple))
    run = pl.pallas_call(
        kernel,
        out_shape=outs,
        in_specs=in_specs,
        out_specs=[VMEM] * len(outs) if many else VMEM,
        scratch_shapes=list(scratch),
        compiler_params=pltpu.CompilerParams(vmem_limit_bytes=mib << 20),
        cost_estimate=pl.CostEstimate(flops=flops, bytes_accessed=bytes_accessed, transcendentals=0),
        name=name,
    )

    def placed(*operands):
        return run(
            *(
                x if spec is VMEM else pltpu.with_memory_space_constraint(x, spec.memory_space)
                for x, spec in zip(operands, in_specs)
            )
        )

    return placed


def rows_of(shape, axis):
    return lax.broadcasted_iota(jnp.int32, shape, axis)


def start_all(pairs, sems):
    copies = [pltpu.make_async_copy(a, b, sems.at[i]) for i, (a, b) in enumerate(pairs)]
    for copy in copies:
        copy.start()
    return copies


def leaf_kernel(cur_h, rad_h, interp_h, phase_h, out, cur, rad, interp, phase, pat, msg, sems):
    pairs = [(cur_h, cur)] + [(rad_h.at[b], rad.at[b]) for b in range(8)] + [(interp_h, interp), (phase_h, phase)]
    copies = start_all(pairs, sems)
    copies[0].wait()
    columns = cur[...].reshape(16, 128).T
    for b in range(8):
        copies[1 + b].wait()
        cr = jnp.broadcast_to(columns[:, 2 * b : 2 * b + 1], (128, 128))
        ci = jnp.broadcast_to(columns[:, 2 * b + 1 : 2 * b + 2], (128, 128))
        for p in range(2):
            rr = rad[b, p, 0]
            ri = rad[b, p, 1]
            pat[pl.ds(16 * p + b, 1), :] = jnp.sum(rr * cr - ri * ci, axis=0, keepdims=True)
            pat[pl.ds(16 * p + 8 + b, 1), :] = jnp.sum(rr * ci + ri * cr, axis=0, keepdims=True)
    copies[9].wait()
    copies[10].wait()
    lifted = jnp.dot(pat[...], interp[...], precision=HIGHEST, preferred_element_type=F32)
    cosine = jnp.cos(phase[...])
    sine = jnp.sin(phase[...])
    for p in range(2):
        yr = lifted[16 * p : 16 * p + 8]
        yi = lifted[16 * p + 8 : 16 * p + 16]
        re = jnp.sum(cosine * yr - sine * yi, axis=0, keepdims=True)
        im = jnp.sum(sine * yr + cosine * yi, axis=0, keepdims=True)
        for c, part in enumerate((re, im)):
            for h in range(2):
                msg[pl.ds(4 * p + 2 * c + h, 1), :] = part[:, 128 * h : 128 * h + 128]
    whole = msg[...]
    for peer in range(8):
        out[peer] = whole


def prep_kernel(
    src_low_h, op_low_h, cnt_low_h, src_up_h, op_up_h, cnt_up_h, tab_low_h, tab_up_h, phase_h, interp_h,
    wa, wb, ua, ub, rot, interp,
    src_low, op_low, cnt_low, src_up, op_up, cnt_up, tab_low, tab_up, phase, ta, tb, code_v, code_s, sem, sems,
):
    clus, samp = place()
    copies = start_all(
        [
            (src_low_h, src_low), (op_low_h, op_low), (cnt_low_h, cnt_low), (src_up_h, src_up),
            (op_up_h, op_up), (cnt_up_h, cnt_up), (phase_h, phase), (tab_low_h, tab_low),
            (tab_up_h, tab_up), (interp_h, interp),
        ],
        sems,
    )
    for copy in copies[:6]:
        copy.wait()
    src = src_low[...]
    used = (rows_of(src.shape, 0) < cnt_low[...]) & ((src >> 3) == clus)
    code = 64 - op_low[...]
    octant = src & 7
    for o in range(8):
        listed = jnp.sum(jnp.where(used & (octant == o), code, 0), axis=0, keepdims=True)
        code_v[pl.ds(o, 1), :] = 64 - listed
    code_v[pl.ds(8, 8), :] = jnp.zeros((8, 256), jnp.int32)
    used_up = (rows_of(src_up.shape, 0) < cnt_up[...]) & (src_up[...] == clus)
    code_v[pl.ds(8, 1), pl.ds(0, 32)] = jnp.sum(jnp.where(used_up, op_up[...] + 1, 0), axis=0, keepdims=True)
    move = pltpu.make_async_copy(code_v, code_s, sem)
    move.start()
    for copy in copies[6:9]:
        copy.wait()
    zero = jnp.zeros((8, 128), F32)
    row = rows_of((8, 128), 0)
    first_half = (row & 1) == 0
    sign_low = jnp.where((row & 2) == 0, -1.0, 1.0).astype(F32)
    sign_up = jnp.where((row & 1) == 0, -1.0, 1.0).astype(F32)[:, :96]
    rot[0] = zero
    rot[1] = zero
    rot[0, :, pl.ds(0, 96)] = jnp.cos(phase[...])
    rot[1, :, pl.ds(0, 96)] = jnp.sin(phase[...])
    ta[64] = zero
    tb[64] = zero

    def expand(n, carry):
        parts = []
        for c in range(2):
            low = jnp.broadcast_to(tab_low[n, pl.ds(c, 1), pl.ds(0, 128)], (8, 128))
            high = jnp.broadcast_to(tab_low[n, pl.ds(c, 1), pl.ds(128, 128)], (8, 128))
            parts.append(jnp.where(first_half, low, high))
        ta[n] = parts[0]
        tb[n] = parts[1] * sign_low
        return carry

    lax.fori_loop(0, 64, expand, 0, unroll=8)
    move.wait()

    def target(t, carry):
        for o in range(8):
            n = code_s[o, t * 8 + samp]
            wa[t, o] = ta[n]
            wb[t, o] = tb[n]
        i = code_s[8, t]
        n = jnp.maximum(i - 1, 0)
        listed = jnp.where(i > 0, 1.0, 0.0).astype(F32)
        ua[t] = zero
        ub[t] = zero
        ua[t, :, pl.ds(0, 96)] = jnp.broadcast_to(tab_up[n, pl.ds(0, 1), :], (8, 96)) * listed
        ub[t, :, pl.ds(0, 96)] = jnp.broadcast_to(tab_up[n, pl.ds(1, 1), :], (8, 96)) * listed * sign_up
        return carry

    lax.fori_loop(0, 32, target, 0, unroll=2)
    for copy in copies[9:]:
        copy.wait()


def middle_kernel(got, interp, wa, wb, ua, ub, rot, arrived, out, upper):
    row = rows_of((8, 128), 0)
    halves = []
    for h in range(2):
        halves.append(
            jnp.concatenate([got[pl.ds(2 * k + h, 8, stride=8), :] for k in range(4)], axis=0)
        )
    lifted = lax.dot_general(
        jnp.concatenate(halves, axis=1), interp[...], (((1,), (1,)), ((), ())),
        precision=HIGHEST, preferred_element_type=F32,
    )
    plain = [got[pl.ds(8 * o, 8), :] for o in range(8)]
    swapped = [
        jnp.where((row & 2) == 0, pltpu.roll(x, 6, 0), pltpu.roll(x, 2, 0)) for x in plain
    ]
    for t in range(32):
        total = wa[t, 0] * plain[0] + wb[t, 0] * swapped[0]
        for o in range(1, 8):
            total += wa[t, o] * plain[o] + wb[t, o] * swapped[o]
        out[3 * t] = total[:4]
        out[3 * t + 1] = total[4:]
    upper[...] = jnp.zeros((8, 128), F32)
    cosine = rot[0][:, :96]
    sine = rot[1][:, :96]
    for p in range(2):
        zr = lifted[16 * p : 16 * p + 8]
        zi = lifted[16 * p + 8 : 16 * p + 16]
        upper[pl.ds(2 * p, 1), pl.ds(0, 96)] = jnp.sum(cosine * zr - sine * zi, axis=0, keepdims=True)
        upper[pl.ds(2 * p + 1, 1), pl.ds(0, 96)] = jnp.sum(sine * zr + cosine * zi, axis=0, keepdims=True)
    up = upper[...]
    up_swapped = jnp.where((row & 1) == 0, pltpu.roll(up, 7, 0), pltpu.roll(up, 1, 0))
    for t in range(32):
        out[3 * t + 2] = (ua[t] * up + ub[t] * up_swapped)[:4]


def near_kernel(cur, even, odd, neighbours_h, count_h, blocks_h, out, blocks, ext, pieces, neighbours, count, sems):
    clus, samp = place()
    base = (clus * 8 + samp) * 8 - 8
    lists = start_all(
        [(cur, ext.at[pl.ds(8, 8)]), (neighbours_h, neighbours), (count_h, count)], sems.at[pl.ds(8, 3)]
    )

    def load(b):
        return pltpu.make_async_copy(blocks_h.at[b], blocks.at[b], sems.at[b])

    for b in range(8):
        load(b).start()
    parity = samp & 1
    ext[pl.ds(16 * (1 - parity), 8)] = even[...]
    ext[pl.ds(16 * parity, 8)] = odd[...]
    pieces[...] = jnp.zeros((2, 256, 256), jnp.bfloat16)
    ones = jnp.ones((16, 256), jnp.bfloat16)
    for one in lists:
        one.wait()

    def finish(slot, b):
        summed = lax.dot_general(
            ones, pieces[slot], (((1,), (1,)), ((), ())), preferred_element_type=F32
        )
        out[b, pl.ds(0, 1), :] = summed[0:1, :128]
        out[b, pl.ds(1, 1), :] = summed[0:1, 128:]

    def box(b, carry):
        slot = b & 1
        finish(1 - slot, jnp.maximum(b - 1, 0))
        xs = []
        for k in range(8):
            i = neighbours[b, k] - base
            keep = jnp.where(k < count[b], 1.0, 0.0).astype(F32)
            xr = ext[i, pl.ds(0, 1), :] * keep
            xi = ext[i, pl.ds(1, 1), :] * keep
            xs.append((jnp.broadcast_to(xr, (8, 128)), jnp.broadcast_to(xi, (8, 128))))
        load(b).wait()
        for it in range(8):
            halves = []
            for half in range(2):
                re = None
                for k, (xr, xi) in enumerate(xs):
                    br = blocks[b, k, 0, pl.ds(16 * it + 8 * half, 8), :]
                    bi = blocks[b, k, 1, pl.ds(16 * it + 8 * half, 8), :]
                    tr = br * xr - bi * xi
                    ti = br * xi + bi * xr
                    re, im = (tr, ti) if re is None else (re + tr, im + ti)
                halves.append((re, im))
            for c in range(2):
                whole = jnp.concatenate([halves[0][c], halves[1][c]], axis=0)
                high = whole.astype(jnp.bfloat16)
                low = (whole - high.astype(F32)).astype(jnp.bfloat16)
                pieces[slot, pl.ds(128 * c + 16 * it, 16), pl.ds(0, 128)] = high
                pieces[slot, pl.ds(128 * c + 16 * it, 16), pl.ds(128, 128)] = low
        return carry

    lax.fori_loop(0, 8, box, 0)
    finish(1, 7)


def final_kernel(got, out_low, out_up):
    sums = [got[k] for k in range(3)]
    for t in range(1, 32):
        for k in range(3):
            sums[k] += got[3 * t + k]
    for p in range(2):
        for c in range(2):
            k = 2 * p + c
            for h in range(2):
                out_low[0, p, pl.ds(c, 1), pl.ds(128 * h, 128)] = sums[p][2 * c + h : 2 * c + h + 1]
            out_up[0, p, pl.ds(c, 1), :] = sums[2][k : k + 1, :96]


def shape(*dims):
    return jax.ShapeDtypeStruct(dims, F32)


def local(
    currents, near_blocks, neighbours, near_count, radiation, interp_leaf, phase_leaf,
    interp_upper, phase_upper, tables_lower, operator_lower, sources_lower, count_lower,
    tables_upper, operator_upper, sources_upper, count_upper,
):
    message = call(
        leaf_kernel, shape(8, 8, 128), [HBM] * 4,
        [
            pltpu.VMEM((8, 2, 128), F32), pltpu.VMEM((8, 2, 2, 128, 128), F32),
            pltpu.VMEM((128, 256), F32), pltpu.VMEM((8, 256), F32),
            pltpu.VMEM((32, 128), F32), pltpu.VMEM((8, 128), F32), pltpu.SemaphoreType.DMA((11,)),
        ],
        flops=4 << 20, bytes_accessed=2 << 20, name="leaf",
    )(currents, radiation, interp_leaf, phase_leaf)
    size = lax.axis_size(CLUS_SAMP)
    own, message = lax.optimization_barrier((currents, message))
    even = lax.ppermute(own, CLUS_SAMP, [(i, i ^ 1) for i in range(size)])
    gathered = lax.all_to_all(message, SAMP, split_axis=0, concat_axis=0, tiled=True)

    wa, wb, ua, ub, rot, interp = call(
        prep_kernel,
        [
            shape(32, 8, 8, 128), shape(32, 8, 8, 128), shape(32, 8, 128), shape(32, 8, 128),
            shape(2, 8, 128), shape(96, 256),
        ],
        [HBM] * 10,
        [
            pltpu.VMEM((16, 256), jnp.int32), pltpu.VMEM((16, 256), jnp.int32), pltpu.VMEM((1, 256), jnp.int32),
            pltpu.VMEM((7, 32), jnp.int32), pltpu.VMEM((7, 32), jnp.int32), pltpu.VMEM((1, 32), jnp.int32),
            pltpu.VMEM((64, 2, 256), F32), pltpu.VMEM((64, 2, 96), F32), pltpu.VMEM((8, 96), F32),
            pltpu.VMEM((65, 8, 128), F32), pltpu.VMEM((65, 8, 128), F32),
            pltpu.VMEM((16, 256), jnp.int32), pltpu.SMEM((16, 256), jnp.int32), pltpu.SemaphoreType.DMA,
            pltpu.SemaphoreType.DMA((10,)),
        ],
        flops=1 << 20, bytes_accessed=4 << 20, name="prep",
    )(
        sources_lower.T, operator_lower.T, count_lower.reshape(1, -1),
        sources_upper.T, operator_upper.T, count_upper.reshape(1, -1),
        tables_lower, tables_upper, phase_upper, interp_upper.T,
    )

    payload = call(
        middle_kernel, shape(96, 4, 128), [VMEM] * 8, [pltpu.VMEM((8, 128), F32)],
        flops=4 << 20, bytes_accessed=3 << 20, name="middle",
    )(gathered.reshape(64, 128), interp, wa, wb, ua, ub, rot, even)
    own, payload = lax.optimization_barrier((currents, payload))
    parts = lax.all_to_all(payload, CLUS, split_axis=0, concat_axis=0, tiled=True)

    odd = lax.ppermute(own, CLUS_SAMP, [(i, ((i + 1) ^ 1) - 1) for i in range(1, size - 1)])
    near_field = call(
        near_kernel, shape(8, 2, 128), [HBM, VMEM, VMEM, HBM, HBM, HBM],
        [
            pltpu.VMEM((8, 8, 2, 128, 128), F32),
            pltpu.VMEM((24, 2, 128), F32),
            pltpu.VMEM((2, 256, 256), jnp.bfloat16),
            pltpu.SMEM((8, 8), jnp.int32),
            pltpu.SMEM((8,), jnp.int32),
            pltpu.SemaphoreType.DMA((11,)),
        ],
        flops=16 << 20, bytes_accessed=8 << 20, name="near",
    )(currents, even, odd, neighbours, near_count, near_blocks)

    incoming_lower, incoming_upper = call(
        final_kernel, [shape(1, 2, 2, 256), shape(1, 2, 2, 96)], [VMEM],
        flops=1 << 17, bytes_accessed=1 << 18, name="final",
    )(parts)
    return near_field, incoming_lower, incoming_upper


def solution(mesh):
    split = Mesh(mesh.devices.reshape(4, 8, 4, 2), CLUS_SAMP)
    whole = P()
    return jax.shard_map(
        local,
        mesh=split,
        in_specs=(
            P(CLUS_SAMP), P(CLUS_SAMP), P(CLUS_SAMP), P(CLUS_SAMP), P(CLUS_SAMP),
            whole, whole, P(None, SAMP), P(None, SAMP),
            whole, whole, whole, whole, P(None, None, SAMP), whole, whole, whole,
        ),
        out_specs=(P(CLUS_SAMP), P(CLUS_SAMP), P(CLUS, None, None, SAMP)),
        check_vma=False,
    )
```

```python
import functools

import jax
import jax.numpy as jnp
from jax import lax
from jax.experimental import pallas as pl
from jax.experimental.pallas import tpu as pltpu
from jax.sharding import Mesh
from jax.sharding import PartitionSpec as P

CLUS = ("clus_0", "clus_1")
SAMP = ("samp_0", "samp_1")
CLUS_SAMP = CLUS + SAMP

HIGHEST = lax.Precision.HIGHEST
F32 = jnp.float32
VMEM = pl.BlockSpec(memory_space=pltpu.VMEM)
SMEM = pl.BlockSpec(memory_space=pltpu.SMEM)
HBM = pl.BlockSpec(memory_space=pltpu.HBM)


def place():
    clus = lax.axis_index("clus_0") * 8 + lax.axis_index("clus_1")
    samp = lax.axis_index("samp_0") * 2 + lax.axis_index("samp_1")
    return clus, samp


def call(kernel, outs, in_specs, scratch=(), mib=16, flops=0, bytes_accessed=0, name=None):
    many = isinstance(outs, (list, tuple))
    run = pl.pallas_call(
        kernel,
        out_shape=outs,
        in_specs=in_specs,
        out_specs=[VMEM] * len(outs) if many else VMEM,
        scratch_shapes=list(scratch),
        compiler_params=pltpu.CompilerParams(vmem_limit_bytes=mib << 20),
        cost_estimate=pl.CostEstimate(flops=flops, bytes_accessed=bytes_accessed, transcendentals=0),
        name=name,
    )

    def placed(*operands):
        return run(
            *(
                x if spec is VMEM else pltpu.with_memory_space_constraint(x, spec.memory_space)
                for x, spec in zip(operands, in_specs)
            )
        )

    return placed


def rows_of(shape, axis):
    return lax.broadcasted_iota(jnp.int32, shape, axis)


def start_all(pairs, sems):
    copies = [pltpu.make_async_copy(a, b, sems.at[i]) for i, (a, b) in enumerate(pairs)]
    for copy in copies:
        copy.start()
    return copies


def leaf_kernel(cur_h, rad_h, interp_h, phase_h, out, cur, rad, interp, phase, pat, msg, sems):
    pairs = [(cur_h, cur)] + [(rad_h.at[b], rad.at[b]) for b in range(8)] + [(interp_h, interp), (phase_h, phase)]
    copies = start_all(pairs, sems)
    copies[0].wait()
    columns = cur[...].reshape(16, 128).T
    for b in range(8):
        copies[1 + b].wait()
        cr = jnp.broadcast_to(columns[:, 2 * b : 2 * b + 1], (128, 128))
        ci = jnp.broadcast_to(columns[:, 2 * b + 1 : 2 * b + 2], (128, 128))
        for p in range(2):
            rr = rad[b, p, 0]
            ri = rad[b, p, 1]
            pat[pl.ds(16 * p + b, 1), :] = jnp.sum(rr * cr - ri * ci, axis=0, keepdims=True)
            pat[pl.ds(16 * p + 8 + b, 1), :] = jnp.sum(rr * ci + ri * cr, axis=0, keepdims=True)
    copies[9].wait()
    copies[10].wait()
    lifted = jnp.dot(pat[...], interp[...], precision=HIGHEST, preferred_element_type=F32)
    cosine = jnp.cos(phase[...])
    sine = jnp.sin(phase[...])
    for p in range(2):
        yr = lifted[16 * p : 16 * p + 8]
        yi = lifted[16 * p + 8 : 16 * p + 16]
        re = jnp.sum(cosine * yr - sine * yi, axis=0, keepdims=True)
        im = jnp.sum(sine * yr + cosine * yi, axis=0, keepdims=True)
        for c, part in enumerate((re, im)):
            for h in range(2):
                msg[pl.ds(4 * p + 2 * c + h, 1), :] = part[:, 128 * h : 128 * h + 128]
    whole = msg[...]
    for peer in range(8):
        out[peer] = whole


def prep_kernel(
    src_low_h, op_low_h, cnt_low_h, src_up_h, op_up_h, cnt_up_h, tab_low_h, tab_up_h, phase_h, interp_h,
    wa, wb, ua, ub, rot, interp,
    src_low, op_low, cnt_low, src_up, op_up, cnt_up, tab_low, tab_up, phase, ta, tb, code_v, code_s, sem, sems,
):
    clus, samp = place()
    copies = start_all(
        [
            (src_low_h, src_low), (op_low_h, op_low), (cnt_low_h, cnt_low), (src_up_h, src_up),
            (op_up_h, op_up), (cnt_up_h, cnt_up), (phase_h, phase), (tab_low_h, tab_low),
            (tab_up_h, tab_up), (interp_h, interp),
        ],
        sems,
    )
    for copy in copies[:6]:
        copy.wait()
    src = src_low[...]
    used = (rows_of(src.shape, 0) < cnt_low[...]) & ((src >> 3) == clus)
    code = 64 - op_low[...]
    octant = src & 7
    for o in range(8):
        listed = jnp.sum(jnp.where(used & (octant == o), code, 0), axis=0, keepdims=True)
        code_v[pl.ds(o, 1), :] = 64 - listed
    code_v[pl.ds(8, 8), :] = jnp.zeros((8, 256), jnp.int32)
    used_up = (rows_of(src_up.shape, 0) < cnt_up[...]) & (src_up[...] == clus)
    code_v[pl.ds(8, 1), pl.ds(0, 32)] = jnp.sum(jnp.where(used_up, op_up[...] + 1, 0), axis=0, keepdims=True)
    move = pltpu.make_async_copy(code_v, code_s, sem)
    move.start()
    for copy in copies[6:9]:
        copy.wait()
    zero = jnp.zeros((8, 128), F32)
    row = rows_of((8, 128), 0)
    first_half = (row & 1) == 0
    sign_low = jnp.where((row & 2) == 0, -1.0, 1.0).astype(F32)
    sign_up = jnp.where((row & 1) == 0, -1.0, 1.0).astype(F32)[:, :96]
    rot[0] = zero
    rot[1] = zero
    rot[0, :, pl.ds(0, 96)] = jnp.cos(phase[...])
    rot[1, :, pl.ds(0, 96)] = jnp.sin(phase[...])
    ta[64] = zero
    tb[64] = zero

    def expand(n, carry):
        parts = []
        for c in range(2):
            low = jnp.broadcast_to(tab_low[n, pl.ds(c, 1), pl.ds(0, 128)], (8, 128))
            high = jnp.broadcast_to(tab_low[n, pl.ds(c, 1), pl.ds(128, 128)], (8, 128))
            parts.append(jnp.where(first_half, low, high))
        ta[n] = parts[0]
        tb[n] = parts[1] * sign_low
        return carry

    lax.fori_loop(0, 64, expand, 0, unroll=8)
    move.wait()

    def target(t, carry):
        for o in range(8):
            n = code_s[o, t * 8 + samp]
            wa[t, o] = ta[n]
            wb[t, o] = tb[n]
        i = code_s[8, t]
        n = jnp.maximum(i - 1, 0)
        listed = jnp.where(i > 0, 1.0, 0.0).astype(F32)
        ua[t] = zero
        ub[t] = zero
        ua[t, :, pl.ds(0, 96)] = jnp.broadcast_to(tab_up[n, pl.ds(0, 1), :], (8, 96)) * listed
        ub[t, :, pl.ds(0, 96)] = jnp.broadcast_to(tab_up[n, pl.ds(1, 1), :], (8, 96)) * listed * sign_up
        return carry

    lax.fori_loop(0, 32, target, 0, unroll=2)
    for copy in copies[9:]:
        copy.wait()


def middle_kernel(got, interp, wa, wb, ua, ub, rot, even, odd, out, upper):
    row = rows_of((8, 128), 0)
    halves = []
    for h in range(2):
        halves.append(
            jnp.concatenate([got[pl.ds(2 * k + h, 8, stride=8), :] for k in range(4)], axis=0)
        )
    lifted = lax.dot_general(
        jnp.concatenate(halves, axis=1), interp[...], (((1,), (1,)), ((), ())),
        precision=HIGHEST, preferred_element_type=F32,
    )
    plain = [got[pl.ds(8 * o, 8), :] for o in range(8)]
    swapped = [
        jnp.where((row & 2) == 0, pltpu.roll(x, 6, 0), pltpu.roll(x, 2, 0)) for x in plain
    ]
    for t in range(32):
        total = wa[t, 0] * plain[0] + wb[t, 0] * swapped[0]
        for o in range(1, 8):
            total += wa[t, o] * plain[o] + wb[t, o] * swapped[o]
        out[3 * t] = total[:4]
        out[3 * t + 1] = total[4:]
    upper[...] = jnp.zeros((8, 128), F32)
    cosine = rot[0][:, :96]
    sine = rot[1][:, :96]
    for p in range(2):
        zr = lifted[16 * p : 16 * p + 8]
        zi = lifted[16 * p + 8 : 16 * p + 16]
        upper[pl.ds(2 * p, 1), pl.ds(0, 96)] = jnp.sum(cosine * zr - sine * zi, axis=0, keepdims=True)
        upper[pl.ds(2 * p + 1, 1), pl.ds(0, 96)] = jnp.sum(sine * zr + cosine * zi, axis=0, keepdims=True)
    up = upper[...]
    up_swapped = jnp.where((row & 1) == 0, pltpu.roll(up, 7, 0), pltpu.roll(up, 1, 0))
    for t in range(32):
        out[3 * t + 2] = (ua[t] * up + ub[t] * up_swapped)[:4]


def near_kernel(cur, even, odd, neighbours_h, count_h, blocks_h, out, blocks, ext, pieces, neighbours, count, sems):
    clus, samp = place()
    base = (clus * 8 + samp) * 8 - 8
    lists = start_all(
        [(cur, ext.at[pl.ds(8, 8)]), (neighbours_h, neighbours), (count_h, count)], sems.at[pl.ds(8, 3)]
    )

    def load(b):
        return pltpu.make_async_copy(blocks_h.at[b], blocks.at[b], sems.at[b])

    for b in range(8):
        load(b).start()
    parity = samp & 1
    ext[pl.ds(16 * (1 - parity), 8)] = even[...]
    ext[pl.ds(16 * parity, 8)] = odd[...]
    pieces[...] = jnp.zeros((2, 256, 256), jnp.bfloat16)
    ones = jnp.ones((16, 256), jnp.bfloat16)
    for one in lists:
        one.wait()

    def finish(slot, b):
        summed = lax.dot_general(
            ones, pieces[slot], (((1,), (1,)), ((), ())), preferred_element_type=F32
        )
        out[b, pl.ds(0, 1), :] = summed[0:1, :128]
        out[b, pl.ds(1, 1), :] = summed[0:1, 128:]

    def box(b, carry):
        slot = b & 1
        finish(1 - slot, jnp.maximum(b - 1, 0))
        xs = []
        for k in range(8):
            i = neighbours[b, k] - base
            keep = jnp.where(k < count[b], 1.0, 0.0).astype(F32)
            xr = ext[i, pl.ds(0, 1), :] * keep
            xi = ext[i, pl.ds(1, 1), :] * keep
            xs.append((jnp.broadcast_to(xr, (8, 128)), jnp.broadcast_to(xi, (8, 128))))
        load(b).wait()
        for it in range(8):
            halves = []
            for half in range(2):
                re = None
                for k, (xr, xi) in enumerate(xs):
                    br = blocks[b, k, 0, pl.ds(16 * it + 8 * half, 8), :]
                    bi = blocks[b, k, 1, pl.ds(16 * it + 8 * half, 8), :]
                    tr = br * xr - bi * xi
                    ti = br * xi + bi * xr
                    re, im = (tr, ti) if re is None else (re + tr, im + ti)
                halves.append((re, im))
            for c in range(2):
                whole = jnp.concatenate([halves[0][c], halves[1][c]], axis=0)
                high = whole.astype(jnp.bfloat16)
                low = (whole - high.astype(F32)).astype(jnp.bfloat16)
                pieces[slot, pl.ds(128 * c + 16 * it, 16), pl.ds(0, 128)] = high
                pieces[slot, pl.ds(128 * c + 16 * it, 16), pl.ds(128, 128)] = low
        return carry

    lax.fori_loop(0, 8, box, 0)
    finish(1, 7)


def final_kernel(got, out_low, out_up):
    sums = [got[k] for k in range(3)]
    for t in range(1, 32):
        for k in range(3):
            sums[k] += got[3 * t + k]
    for p in range(2):
        for c in range(2):
            k = 2 * p + c
            for h in range(2):
                out_low[0, p, pl.ds(c, 1), pl.ds(128 * h, 128)] = sums[p][2 * c + h : 2 * c + h + 1]
            out_up[0, p, pl.ds(c, 1), :] = sums[2][k : k + 1, :96]


def shape(*dims):
    return jax.ShapeDtypeStruct(dims, F32)


def local(
    currents, near_blocks, neighbours, near_count, radiation, interp_leaf, phase_leaf,
    interp_upper, phase_upper, tables_lower, operator_lower, sources_lower, count_lower,
    tables_upper, operator_upper, sources_upper, count_upper,
):
    message = call(
        leaf_kernel, shape(8, 8, 128), [HBM] * 4,
        [
            pltpu.VMEM((8, 2, 128), F32), pltpu.VMEM((8, 2, 2, 128, 128), F32),
            pltpu.VMEM((128, 256), F32), pltpu.VMEM((8, 256), F32),
            pltpu.VMEM((32, 128), F32), pltpu.VMEM((8, 128), F32), pltpu.SemaphoreType.DMA((11,)),
        ],
        flops=4 << 20, bytes_accessed=2 << 20, name="leaf",
    )(currents, radiation, interp_leaf, phase_leaf)
    size = lax.axis_size(CLUS_SAMP)
    own, message = lax.optimization_barrier((currents, message))
    even = lax.ppermute(own, CLUS_SAMP, [(i, i ^ 1) for i in range(size)])
    odd = lax.ppermute(own, CLUS_SAMP, [(i, ((i + 1) ^ 1) - 1) for i in range(1, size - 1)])
    gathered = lax.all_to_all(message, SAMP, split_axis=0, concat_axis=0, tiled=True)

    wa, wb, ua, ub, rot, interp = call(
        prep_kernel,
        [
            shape(32, 8, 8, 128), shape(32, 8, 8, 128), shape(32, 8, 128), shape(32, 8, 128),
            shape(2, 8, 128), shape(96, 256),
        ],
        [HBM] * 10,
        [
            pltpu.VMEM((16, 256), jnp.int32), pltpu.VMEM((16, 256), jnp.int32), pltpu.VMEM((1, 256), jnp.int32),
            pltpu.VMEM((7, 32), jnp.int32), pltpu.VMEM((7, 32), jnp.int32), pltpu.VMEM((1, 32), jnp.int32),
            pltpu.VMEM((64, 2, 256), F32), pltpu.VMEM((64, 2, 96), F32), pltpu.VMEM((8, 96), F32),
            pltpu.VMEM((65, 8, 128), F32), pltpu.VMEM((65, 8, 128), F32),
            pltpu.VMEM((16, 256), jnp.int32), pltpu.SMEM((16, 256), jnp.int32), pltpu.SemaphoreType.DMA,
            pltpu.SemaphoreType.DMA((10,)),
        ],
        flops=1 << 20, bytes_accessed=4 << 20, name="prep",
    )(
        sources_lower.T, operator_lower.T, count_lower.reshape(1, -1),
        sources_upper.T, operator_upper.T, count_upper.reshape(1, -1),
        tables_lower, tables_upper, phase_upper, interp_upper.T,
    )

    payload = call(
        middle_kernel, shape(96, 4, 128), [VMEM] * 9, [pltpu.VMEM((8, 128), F32)],
        flops=4 << 20, bytes_accessed=3 << 20, name="middle",
    )(gathered.reshape(64, 128), interp, wa, wb, ua, ub, rot, even, odd)
    parts = lax.all_to_all(payload, CLUS, split_axis=0, concat_axis=0, tiled=True)

    near_field = call(
        near_kernel, shape(8, 2, 128), [HBM, VMEM, VMEM, HBM, HBM, HBM],
        [
            pltpu.VMEM((8, 8, 2, 128, 128), F32),
            pltpu.VMEM((24, 2, 128), F32),
            pltpu.VMEM((2, 256, 256), jnp.bfloat16),
            pltpu.SMEM((8, 8), jnp.int32),
            pltpu.SMEM((8,), jnp.int32),
            pltpu.SemaphoreType.DMA((11,)),
        ],
        flops=16 << 20, bytes_accessed=8 << 20, name="near",
    )(currents, even, odd, neighbours, near_count, near_blocks)

    incoming_lower, incoming_upper = call(
        final_kernel, [shape(1, 2, 2, 256), shape(1, 2, 2, 96)], [VMEM],
        flops=1 << 17, bytes_accessed=1 << 18, name="final",
    )(parts)
    return near_field, incoming_lower, incoming_upper


def solution(mesh):
    split = Mesh(mesh.devices.reshape(4, 8, 4, 2), CLUS_SAMP)
    whole = P()
    return jax.shard_map(
        local,
        mesh=split,
        in_specs=(
            P(CLUS_SAMP), P(CLUS_SAMP), P(CLUS_SAMP), P(CLUS_SAMP), P(CLUS_SAMP),
            whole, whole, P(None, SAMP), P(None, SAMP),
            whole, whole, whole, whole, P(None, None, SAMP), whole, whole, whole,
        ),
        out_specs=(P(CLUS_SAMP), P(CLUS_SAMP), P(CLUS, None, None, SAMP)),
        check_vma=False,
    )
```

```python
import jax
import jax.numpy as jnp
from jax import lax
from jax.experimental import pallas as pl
from jax.experimental.pallas import tpu as pltpu
from jax.sharding import Mesh
from jax.sharding import PartitionSpec as P

CLUS = ("clus_0", "clus_1")
SAMP = ("samp_0", "samp_1")
CLUS_SAMP = CLUS + SAMP

F32 = jnp.float32
BF16 = jnp.bfloat16
VMEM = pl.BlockSpec(memory_space=pltpu.VMEM)
SMEM = pl.BlockSpec(memory_space=pltpu.SMEM)
HBM = pl.BlockSpec(memory_space=pltpu.HBM)


def place():
    clus = lax.axis_index("clus_0") * 8 + lax.axis_index("clus_1")
    samp = lax.axis_index("samp_0") * 2 + lax.axis_index("samp_1")
    return clus, samp


def call(kernel, outs, in_specs, scratch=(), mib=16, flops=0, bytes_accessed=0):
    many = isinstance(outs, (list, tuple))
    run = pl.pallas_call(
        kernel,
        out_shape=outs,
        in_specs=in_specs,
        out_specs=[VMEM] * len(outs) if many else VMEM,
        scratch_shapes=list(scratch),
        compiler_params=pltpu.CompilerParams(vmem_limit_bytes=mib << 20),
        cost_estimate=pl.CostEstimate(flops=flops, bytes_accessed=bytes_accessed, transcendentals=0),
    )

    def placed(*operands):
        return run(
            *(
                x if spec is VMEM else pltpu.with_memory_space_constraint(x, spec.memory_space)
                for x, spec in zip(operands, in_specs)
            )
        )

    return placed


def rows_of(shape, axis):
    return lax.broadcasted_iota(jnp.int32, shape, axis)


def start_all(pairs, sems):
    copies = [pltpu.make_async_copy(a, b, sems.at[i]) for i, (a, b) in enumerate(pairs)]
    for copy in copies:
        copy.start()
    return copies


def pieces_of(x):
    high = x.astype(BF16)
    return high, (x - high.astype(F32)).astype(BF16)


def rotated(cosine, sine, y, p):
    yr = y[16 * p : 16 * p + 8]
    yi = y[16 * p + 8 : 16 * p + 16]
    re = jnp.sum(cosine * yr - sine * yi, axis=0, keepdims=True)
    im = jnp.sum(sine * yr + cosine * yi, axis=0, keepdims=True)
    return re, im


def leaf_kernel(
    cur_h, rad_h, interp_h, phase_h, src_low_h, op_low_h, cnt_low_h, src_up_h, op_up_h, cnt_up_h,
    tab_low_h, tab_up_h, phase_up_h, interp_up_h,
    out, code_v, ta, tb, tab_up, rot, weights,
    cur, rad, interp, phase, src_low, op_low, cnt_low, src_up, op_up, cnt_up, tab_low, phase_up, interp_up,
    pat, msg, sems,
):
    clus, _ = place()
    copies = start_all(
        [
            (src_low_h, src_low), (op_low_h, op_low), (cnt_low_h, cnt_low), (src_up_h, src_up),
            (op_up_h, op_up), (cnt_up_h, cnt_up), (cur_h, cur), (phase_h, phase), (interp_h, interp),
            (tab_low_h, tab_low), (tab_up_h, tab_up), (phase_up_h, phase_up), (interp_up_h, interp_up),
        ]
        + [(rad_h.at[b], rad.at[b]) for b in range(8)],
        sems,
    )
    for copy in copies[:13]:
        copy.wait()
    zero = jnp.zeros((8, 128), F32)
    row = rows_of((8, 128), 0)
    first_half = (row & 1) == 0
    sign_low = jnp.where((row & 2) == 0, -1.0, 1.0).astype(F32)
    src = src_low[...]
    used = (rows_of(src.shape, 0) < cnt_low[...]) & ((src >> 3) == clus)
    code = 64 - op_low[...]
    octant = src & 7
    for o in range(8):
        listed = jnp.sum(jnp.where(used & (octant == o), code, 0), axis=0, keepdims=True)
        code_v[pl.ds(o, 1), :] = 64 - listed
    code_v[pl.ds(8, 8), :] = jnp.zeros((8, 256), jnp.int32)
    used_up = (rows_of(src_up.shape, 0) < cnt_up[...]) & (src_up[...] == clus)
    code_v[pl.ds(8, 1), pl.ds(0, 32)] = jnp.sum(jnp.where(used_up, op_up[...] + 1, 0), axis=0, keepdims=True)
    ta[64] = zero
    tb[64] = zero

    def expand(n, carry):
        parts = []
        for c in range(2):
            low = jnp.broadcast_to(tab_low[n, pl.ds(c, 1), pl.ds(0, 128)], (8, 128))
            high = jnp.broadcast_to(tab_low[n, pl.ds(c, 1), pl.ds(128, 128)], (8, 128))
            parts.append(jnp.where(first_half, low, high))
        ta[n] = parts[0]
        tb[n] = parts[1] * sign_low
        return carry

    lax.fori_loop(0, 64, expand, 0, unroll=8)
    rot[0] = zero
    rot[1] = zero
    rot[0, :, pl.ds(0, 96)] = jnp.cos(phase_up[...])
    rot[1, :, pl.ds(0, 96)] = jnp.sin(phase_up[...])
    high, low = pieces_of(interp_up[...])
    weights[...] = jnp.concatenate([high, low, high], axis=1)
    high, low = pieces_of(interp[...])
    weights_leaf = jnp.concatenate([high, low, high], axis=0)
    cosine = jnp.cos(phase[...])
    sine = jnp.sin(phase[...])
    own = cur[...].reshape(16, 128)
    for peer in range(8):
        out[peer, pl.ds(8, 16), :] = own
    columns = own.T
    for b in range(8):
        copies[13 + b].wait()
        cr = jnp.broadcast_to(columns[:, 2 * b : 2 * b + 1], (128, 128))
        ci = jnp.broadcast_to(columns[:, 2 * b + 1 : 2 * b + 2], (128, 128))
        for p in range(2):
            rr = rad[b, p, 0]
            ri = rad[b, p, 1]
            pat[pl.ds(16 * p + b, 1), :] = jnp.sum(rr * cr - ri * ci, axis=0, keepdims=True)
            pat[pl.ds(16 * p + 8 + b, 1), :] = jnp.sum(rr * ci + ri * cr, axis=0, keepdims=True)
    high, low = pieces_of(pat[...])
    lifted = jnp.dot(
        jnp.concatenate([high, high, low], axis=1), weights_leaf, preferred_element_type=F32
    )
    for p in range(2):
        for c, part in enumerate(rotated(cosine, sine, lifted, p)):
            for h in range(2):
                msg[pl.ds(4 * p + 2 * c + h, 1), :] = part[:, 128 * h : 128 * h + 128]
    whole = msg[...]
    for peer in range(8):
        out[peer, pl.ds(0, 8), :] = whole


def prep_kernel(code_v, ta, tb, tab_up, wa, wb, ua, ub, code_s, sem):
    _, samp = place()
    move = pltpu.make_async_copy(code_v, code_s, sem)
    move.start()
    row = rows_of((8, 128), 0)
    sign_up = jnp.where((row & 1) == 0, -1.0, 1.0).astype(F32)[:, :96]
    ua[...] = jnp.zeros((32, 8, 128), F32)
    ub[...] = jnp.zeros((32, 8, 128), F32)
    move.wait()

    def target(t, carry):
        for o in range(8):
            n = code_s[o, t * 8 + samp]
            wa[t, o] = ta[n]
            wb[t, o] = tb[n]
        i = code_s[8, t]
        n = jnp.maximum(i - 1, 0)
        listed = jnp.where(i > 0, 1.0, 0.0).astype(F32)
        ua[t, :, pl.ds(0, 96)] = jnp.broadcast_to(tab_up[n, pl.ds(0, 1), :], (8, 96)) * listed
        ub[t, :, pl.ds(0, 96)] = jnp.broadcast_to(tab_up[n, pl.ds(1, 1), :], (8, 96)) * listed * sign_up
        return carry

    lax.fori_loop(0, 32, target, 0, unroll=2)


def middle_kernel(got, weights, wa, wb, ua, ub, rot, out, upper):
    row = rows_of((8, 128), 0)
    halves = []
    for h in range(2):
        halves.append(
            jnp.concatenate([got[pl.ds(2 * k + h, 8, stride=24), :] for k in range(4)], axis=0)
        )
    high, low = pieces_of(jnp.concatenate(halves, axis=1))
    lifted = lax.dot_general(
        jnp.concatenate([high, high, low], axis=1), weights[...], (((1,), (1,)), ((), ())),
        preferred_element_type=F32,
    )
    plain = [got[pl.ds(24 * o, 8), :] for o in range(8)]
    swapped = [
        jnp.where((row & 2) == 0, pltpu.roll(x, 6, 0), pltpu.roll(x, 2, 0)) for x in plain
    ]
    for t in range(32):
        total = wa[t, 0] * plain[0] + wb[t, 0] * swapped[0]
        for o in range(1, 8):
            total += wa[t, o] * plain[o] + wb[t, o] * swapped[o]
        out[3 * t] = total[:4]
        out[3 * t + 1] = total[4:]
    upper[...] = jnp.zeros((8, 128), F32)
    cosine = rot[0][:, :96]
    sine = rot[1][:, :96]
    for p in range(2):
        for c, part in enumerate(rotated(cosine, sine, lifted, p)):
            upper[pl.ds(2 * p + c, 1), pl.ds(0, 96)] = part
    up = upper[...]
    up_swapped = jnp.where((row & 1) == 0, pltpu.roll(up, 7, 0), pltpu.roll(up, 1, 0))
    for t in range(32):
        out[3 * t + 2] = (ua[t] * up + ub[t] * up_swapped)[:4]


def near_kernel(got, cross, neighbours_h, count_h, blocks_h, out, blocks, ext, pieces, neighbours, count, sems):
    clus, samp = place()
    base = (clus * 8 + samp) * 8 - 8
    lists = start_all([(neighbours_h, neighbours), (count_h, count)], sems.at[pl.ds(8, 2)])

    def load(b):
        return pltpu.make_async_copy(blocks_h.at[b], blocks.at[b], sems.at[b])

    for b in range(8):
        load(b).start()
    outside = cross[...].reshape(16, 128)
    before = got[jnp.maximum(samp - 1, 0), pl.ds(8, 16), :]
    after = got[jnp.minimum(samp + 1, 7), pl.ds(8, 16), :]
    ext[pl.ds(0, 16), :] = jnp.where(samp > 0, before, outside)
    ext[pl.ds(16, 16), :] = got[samp, pl.ds(8, 16), :]
    ext[pl.ds(32, 16), :] = jnp.where(samp < 7, after, outside)
    pieces[...] = jnp.zeros((2, 256, 256), BF16)
    ones = jnp.ones((16, 256), BF16)
    for one in lists:
        one.wait()

    def finish(slot, b):
        summed = lax.dot_general(
            ones, pieces[slot], (((1,), (1,)), ((), ())), preferred_element_type=F32
        )
        out[b, pl.ds(0, 1), :] = summed[0:1, :128]
        out[b, pl.ds(1, 1), :] = summed[0:1, 128:]

    def box(b, carry):
        slot = b & 1
        finish(1 - slot, jnp.maximum(b - 1, 0))
        xs = []
        for k in range(8):
            i = neighbours[b, k] - base
            keep = jnp.where(k < count[b], 1.0, 0.0).astype(F32)
            xr = ext[pl.ds(2 * i, 1), :] * keep
            xi = ext[pl.ds(2 * i + 1, 1), :] * keep
            xs.append((jnp.broadcast_to(xr, (8, 128)), jnp.broadcast_to(xi, (8, 128))))
        load(b).wait()
        for it in range(8):
            halves = []
            for half in range(2):
                re = None
                for k, (xr, xi) in enumerate(xs):
                    br = blocks[b, k, 0, pl.ds(16 * it + 8 * half, 8), :]
                    bi = blocks[b, k, 1, pl.ds(16 * it + 8 * half, 8), :]
                    tr = br * xr - bi * xi
                    ti = br * xi + bi * xr
                    re, im = (tr, ti) if re is None else (re + tr, im + ti)
                halves.append((re, im))
            for c in range(2):
                whole = jnp.concatenate([halves[0][c], halves[1][c]], axis=0)
                high = whole.astype(BF16)
                low = (whole - high.astype(F32)).astype(BF16)
                pieces[slot, pl.ds(128 * c + 16 * it, 16), pl.ds(0, 128)] = high
                pieces[slot, pl.ds(128 * c + 16 * it, 16), pl.ds(128, 128)] = low
        return carry

    lax.fori_loop(0, 8, box, 0)
    finish(1, 7)


def final_kernel(got, out_low, out_up):
    sums = [got[k] for k in range(3)]
    for t in range(1, 32):
        for k in range(3):
            sums[k] += got[3 * t + k]
    for p in range(2):
        for c in range(2):
            k = 2 * p + c
            for h in range(2):
                out_low[0, p, pl.ds(c, 1), pl.ds(128 * h, 128)] = sums[p][2 * c + h : 2 * c + h + 1]
            out_up[0, p, pl.ds(c, 1), :] = sums[2][k : k + 1, :96]


def shape(*dims):
    return jax.ShapeDtypeStruct(dims, F32)


def local(
    currents, near_blocks, neighbours, near_count, radiation, interp_leaf, phase_leaf,
    interp_upper, phase_upper, tables_lower, operator_lower, sources_lower, count_lower,
    tables_upper, operator_upper, sources_upper, count_upper,
):
    ints = jnp.int32
    message, code, ta, tb, tab_up, rot, weights = call(
        leaf_kernel,
        [
            shape(8, 24, 128), jax.ShapeDtypeStruct((16, 256), ints), shape(65, 8, 128), shape(65, 8, 128),
            shape(64, 2, 96), shape(2, 8, 128), jax.ShapeDtypeStruct((96, 768), BF16),
        ],
        [HBM] * 14,
        [
            pltpu.VMEM((8, 2, 128), F32), pltpu.VMEM((8, 2, 2, 128, 128), F32),
            pltpu.VMEM((128, 256), F32), pltpu.VMEM((8, 256), F32),
            pltpu.VMEM((16, 256), ints), pltpu.VMEM((16, 256), ints), pltpu.VMEM((1, 256), ints),
            pltpu.VMEM((7, 32), ints), pltpu.VMEM((7, 32), ints), pltpu.VMEM((1, 32), ints),
            pltpu.VMEM((64, 2, 256), F32), pltpu.VMEM((8, 96), F32), pltpu.VMEM((96, 256), F32),
            pltpu.VMEM((32, 128), F32), pltpu.VMEM((8, 128), F32), pltpu.SemaphoreType.DMA((21,)),
        ],
        flops=4 << 20, bytes_accessed=3 << 20,
    )(
        currents, radiation, interp_leaf, phase_leaf,
        sources_lower.T, operator_lower.T, count_lower.reshape(1, -1),
        sources_upper.T, operator_upper.T, count_upper.reshape(1, -1),
        tables_lower, tables_upper, phase_upper, interp_upper.T,
    )
    own, message = lax.optimization_barrier((currents, message))
    gathered = lax.all_to_all(message, SAMP, split_axis=0, concat_axis=0, tiled=True)
    size = lax.axis_size(CLUS_SAMP)
    ends = range(7, size - 1, 8)
    cross = lax.ppermute(own, CLUS_SAMP, [(i, i + 1) for i in ends] + [(i + 1, i) for i in ends])

    wa, wb, ua, ub = call(
        prep_kernel,
        [shape(32, 8, 8, 128), shape(32, 8, 8, 128), shape(32, 8, 128), shape(32, 8, 128)],
        [VMEM] * 4,
        [pltpu.SMEM((16, 256), ints), pltpu.SemaphoreType.DMA],
        flops=1 << 20, bytes_accessed=4 << 20,
    )(code, ta, tb, tab_up)

    payload = call(
        middle_kernel, shape(96, 4, 128), [VMEM] * 7, [pltpu.VMEM((8, 128), F32)],
        flops=4 << 20, bytes_accessed=3 << 20,
    )(gathered.reshape(192, 128), weights, wa, wb, ua, ub, rot)
    parts = lax.all_to_all(payload, CLUS, split_axis=0, concat_axis=0, tiled=True)

    near_field = call(
        near_kernel, shape(8, 2, 128), [VMEM, VMEM, HBM, HBM, HBM],
        [
            pltpu.VMEM((8, 8, 2, 128, 128), F32),
            pltpu.VMEM((48, 128), F32),
            pltpu.VMEM((2, 256, 256), BF16),
            pltpu.SMEM((8, 8), ints),
            pltpu.SMEM((8,), ints),
            pltpu.SemaphoreType.DMA((10,)),
        ],
        flops=16 << 20, bytes_accessed=8 << 20,
    )(gathered, cross, neighbours, near_count, near_blocks)

    incoming_lower, incoming_upper = call(
        final_kernel, [shape(1, 2, 2, 256), shape(1, 2, 2, 96)], [VMEM],
        flops=1 << 17, bytes_accessed=1 << 18,
    )(parts)
    return near_field, incoming_lower, incoming_upper


def solution(mesh):
    split = Mesh(mesh.devices.reshape(4, 8, 4, 2), CLUS_SAMP)
    whole = P()
    return jax.shard_map(
        local,
        mesh=split,
        in_specs=(
            P(CLUS_SAMP), P(CLUS_SAMP), P(CLUS_SAMP), P(CLUS_SAMP), P(CLUS_SAMP),
            whole, whole, P(None, SAMP), P(None, SAMP),
            whole, whole, whole, whole, P(None, None, SAMP), whole, whole, whole,
        ),
        out_specs=(P(CLUS_SAMP), P(CLUS_SAMP), P(CLUS, None, None, SAMP)),
        check_vma=False,
    )
```

```python
import jax
import jax.numpy as jnp
from jax import lax
from jax.experimental import pallas as pl
from jax.experimental.pallas import tpu as pltpu
from jax.sharding import Mesh
from jax.sharding import PartitionSpec as P

CLUS = ("clus_0", "clus_1")
SAMP = ("samp_0", "samp_1")
CLUS_SAMP = CLUS + SAMP

F32 = jnp.float32
CHUNKS = 4
BF16 = jnp.bfloat16
VMEM = pl.BlockSpec(memory_space=pltpu.VMEM)
SMEM = pl.BlockSpec(memory_space=pltpu.SMEM)
HBM = pl.BlockSpec(memory_space=pltpu.HBM)


def place():
    clus = lax.axis_index("clus_0") * 8 + lax.axis_index("clus_1")
    samp = lax.axis_index("samp_0") * 2 + lax.axis_index("samp_1")
    return clus, samp


def call(kernel, outs, in_specs, scratch=(), mib=16, flops=0, bytes_accessed=0, first=None):
    many = isinstance(outs, (list, tuple))
    run = pl.pallas_call(
        kernel,
        out_shape=outs,
        in_specs=in_specs,
        out_specs=[first or VMEM] + [VMEM] * (len(outs) - 1) if many else first or VMEM,
        scratch_shapes=list(scratch),
        compiler_params=pltpu.CompilerParams(vmem_limit_bytes=mib << 20),
        cost_estimate=pl.CostEstimate(flops=flops, bytes_accessed=bytes_accessed, transcendentals=0),
    )

    def placed(*operands):
        return run(
            *(
                x if spec is VMEM else pltpu.with_memory_space_constraint(x, spec.memory_space)
                for x, spec in zip(operands, in_specs)
            )
        )

    return placed


def rows_of(shape, axis):
    return lax.broadcasted_iota(jnp.int32, shape, axis)


def start_all(pairs, sems):
    copies = [pltpu.make_async_copy(a, b, sems.at[i]) for i, (a, b) in enumerate(pairs)]
    for copy in copies:
        copy.start()
    return copies


def pieces_of(x):
    high = x.astype(BF16)
    return high, (x - high.astype(F32)).astype(BF16)


def rotated(cosine, sine, y, p):
    yr = y[16 * p : 16 * p + 8]
    yi = y[16 * p + 8 : 16 * p + 16]
    re = jnp.sum(cosine * yr - sine * yi, axis=0, keepdims=True)
    im = jnp.sum(sine * yr + cosine * yi, axis=0, keepdims=True)
    return re, im


def leaf_kernel(
    cur_h, rad_h, interp_h, phase_h, in0, in1, in2, in3, in4, in5, in6, in7, in8, in9,
    out, to0, to1, to2, to3, to4, to5, to6, to7, to8, to9,
    cur, rad, interp, phase, pat, msg, sems, later_sems,
):
    later_h = [in0, in1, in2, in3, in4, in5, in6, in7, in8, in9]
    later = [to0, to1, to2, to3, to4, to5, to6, to7, to8, to9]
    chunk = 8 // CHUNKS
    spans = [pl.ds(chunk * i, chunk) for i in range(CHUNKS)]
    pairs = [(cur_h, cur)] + [(rad_h.at[span], rad.at[span]) for span in spans]
    copies = start_all(pairs + [(interp_h, interp), (phase_h, phase)], sems)
    others = start_all(list(zip(later_h, later)), later_sems)
    copies[0].wait()
    own = cur[...].reshape(16, 128)
    msg[pl.ds(8, 16), :] = own
    sent = [
        pltpu.make_async_copy(msg.at[pl.ds(8, 16)], out.at[peer, pl.ds(8, 16)], sems.at[21 + peer])
        for peer in range(8)
    ]
    for copy in sent:
        copy.start()
    columns = own.T
    for b in range(8):
        if b % chunk == 0:
            copies[1 + b // chunk].wait()
        cr = jnp.broadcast_to(columns[:, 2 * b : 2 * b + 1], (128, 128))
        ci = jnp.broadcast_to(columns[:, 2 * b + 1 : 2 * b + 2], (128, 128))
        for p in range(2):
            rr = rad[b, p, 0]
            ri = rad[b, p, 1]
            pat[pl.ds(16 * p + b, 1), :] = jnp.sum(rr * cr - ri * ci, axis=0, keepdims=True)
            pat[pl.ds(16 * p + 8 + b, 1), :] = jnp.sum(rr * ci + ri * cr, axis=0, keepdims=True)
    copies[-2].wait()
    copies[-1].wait()
    high, low = pieces_of(interp[...])
    weights_leaf = jnp.concatenate([high, low, high], axis=0)
    cosine = jnp.cos(phase[...])
    sine = jnp.sin(phase[...])
    high, low = pieces_of(pat[...])
    lifted = jnp.dot(
        jnp.concatenate([high, high, low], axis=1), weights_leaf, preferred_element_type=F32
    )
    for p in range(2):
        for c, part in enumerate(rotated(cosine, sine, lifted, p)):
            for h in range(2):
                msg[pl.ds(4 * p + 2 * c + h, 1), :] = part[:, 128 * h : 128 * h + 128]
    last = [
        pltpu.make_async_copy(msg.at[pl.ds(0, 8)], out.at[peer, pl.ds(0, 8)], sems.at[29 + peer])
        for peer in range(8)
    ]
    for copy in last:
        copy.start()
    for copy in others + sent + last:
        copy.wait()


def prep_kernel(
    src_low, op_low, cnt_low, src_up, op_up, cnt_up, tab_low, tab_up, phase_up, interp_up,
    wa, wb, ua, ub, rot, weights, code_v, ta, tb, code_s, sem,
):
    clus, samp = place()
    zero = jnp.zeros((8, 128), F32)
    row = rows_of((8, 128), 0)
    first_half = (row & 1) == 0
    sign_low = jnp.where((row & 2) == 0, -1.0, 1.0).astype(F32)
    sign_up = jnp.where((row & 1) == 0, -1.0, 1.0).astype(F32)[:, :96]
    code_v[pl.ds(8, 8), :] = jnp.zeros((8, 256), jnp.int32)
    src = src_low[...]
    used = (rows_of(src.shape, 0) < cnt_low[...]) & ((src >> 3) == clus)
    code = 64 - op_low[...]
    octant = src & 7
    for o in range(8):
        listed = jnp.sum(jnp.where(used & (octant == o), code, 0), axis=0, keepdims=True)
        code_v[pl.ds(o, 1), :] = 64 - listed
    used_up = (rows_of(src_up.shape, 0) < cnt_up[...]) & (src_up[...] == clus)
    code_v[pl.ds(8, 1), pl.ds(0, 32)] = jnp.sum(jnp.where(used_up, op_up[...] + 1, 0), axis=0, keepdims=True)
    move = pltpu.make_async_copy(code_v, code_s, sem)
    move.start()
    ta[64] = zero
    tb[64] = zero
    rot[0] = zero
    rot[1] = zero
    ua[...] = jnp.zeros((32, 8, 128), F32)
    ub[...] = jnp.zeros((32, 8, 128), F32)

    def expand(n, carry):
        parts = []
        for c in range(2):
            low = jnp.broadcast_to(tab_low[n, pl.ds(c, 1), pl.ds(0, 128)], (8, 128))
            high = jnp.broadcast_to(tab_low[n, pl.ds(c, 1), pl.ds(128, 128)], (8, 128))
            parts.append(jnp.where(first_half, low, high))
        ta[n] = parts[0]
        tb[n] = parts[1] * sign_low
        return carry

    lax.fori_loop(0, 64, expand, 0, unroll=8)
    rot[0, :, pl.ds(0, 96)] = jnp.cos(phase_up[...])
    rot[1, :, pl.ds(0, 96)] = jnp.sin(phase_up[...])
    high, low = pieces_of(interp_up[...])
    weights[...] = jnp.concatenate([high, low, high], axis=1)
    move.wait()

    def target(t, carry):
        for o in range(8):
            n = code_s[o, t * 8 + samp]
            wa[t, o] = ta[n]
            wb[t, o] = tb[n]
        i = code_s[8, t]
        n = jnp.maximum(i - 1, 0)
        listed = jnp.where(i > 0, 1.0, 0.0).astype(F32)
        ua[t, :, pl.ds(0, 96)] = jnp.broadcast_to(tab_up[n, pl.ds(0, 1), :], (8, 96)) * listed
        ub[t, :, pl.ds(0, 96)] = jnp.broadcast_to(tab_up[n, pl.ds(1, 1), :], (8, 96)) * listed * sign_up
        return carry

    lax.fori_loop(0, 32, target, 0, unroll=4)


def middle_kernel(got, weights, wa, wb, ua, ub, rot, out, upper):
    row = rows_of((8, 128), 0)
    halves = []
    for h in range(2):
        halves.append(
            jnp.concatenate([got[pl.ds(2 * k + h, 8, stride=24), :] for k in range(4)], axis=0)
        )
    high, low = pieces_of(jnp.concatenate(halves, axis=1))
    lifted = lax.dot_general(
        jnp.concatenate([high, high, low], axis=1), weights[...], (((1,), (1,)), ((), ())),
        preferred_element_type=F32,
    )
    plain = [got[pl.ds(24 * o, 8), :] for o in range(8)]
    swapped = [
        jnp.where((row & 2) == 0, pltpu.roll(x, 6, 0), pltpu.roll(x, 2, 0)) for x in plain
    ]
    for t in range(32):
        total = wa[t, 0] * plain[0] + wb[t, 0] * swapped[0]
        for o in range(1, 8):
            total += wa[t, o] * plain[o] + wb[t, o] * swapped[o]
        out[3 * t] = total[:4]
        out[3 * t + 1] = total[4:]
    upper[...] = jnp.zeros((8, 128), F32)
    cosine = rot[0][:, :96]
    sine = rot[1][:, :96]
    for p in range(2):
        for c, part in enumerate(rotated(cosine, sine, lifted, p)):
            upper[pl.ds(2 * p + c, 1), pl.ds(0, 96)] = part
    up = upper[...]
    up_swapped = jnp.where((row & 1) == 0, pltpu.roll(up, 7, 0), pltpu.roll(up, 1, 0))
    for t in range(32):
        out[3 * t + 2] = (ua[t] * up + ub[t] * up_swapped)[:4]


def near_kernel(got, cross, neighbours_h, count_h, blocks_h, out, blocks, ext, pieces, neighbours, count, sems):
    clus, samp = place()
    base = (clus * 8 + samp) * 8 - 8
    lists = start_all([(neighbours_h, neighbours), (count_h, count)], sems.at[pl.ds(8, 2)])

    def load(b):
        return pltpu.make_async_copy(blocks_h.at[b], blocks.at[b], sems.at[b])

    for b in range(8):
        load(b).start()
    outside = cross[...].reshape(16, 128)
    before = got[jnp.maximum(samp - 1, 0), pl.ds(8, 16), :]
    after = got[jnp.minimum(samp + 1, 7), pl.ds(8, 16), :]
    ext[pl.ds(0, 16), :] = jnp.where(samp > 0, before, outside)
    ext[pl.ds(16, 16), :] = got[samp, pl.ds(8, 16), :]
    ext[pl.ds(32, 16), :] = jnp.where(samp < 7, after, outside)
    pieces[...] = jnp.zeros((2, 256, 256), BF16)
    ones = jnp.ones((16, 256), BF16)
    for one in lists:
        one.wait()

    def finish(slot, b):
        summed = lax.dot_general(
            ones, pieces[slot], (((1,), (1,)), ((), ())), preferred_element_type=F32
        )
        out[b, pl.ds(0, 1), :] = summed[0:1, :128]
        out[b, pl.ds(1, 1), :] = summed[0:1, 128:]

    def box(b, carry):
        slot = b & 1
        finish(1 - slot, jnp.maximum(b - 1, 0))
        xs = []
        for k in range(8):
            i = neighbours[b, k] - base
            keep = jnp.where(k < count[b], 1.0, 0.0).astype(F32)
            xr = ext[pl.ds(2 * i, 1), :] * keep
            xi = ext[pl.ds(2 * i + 1, 1), :] * keep
            xs.append((jnp.broadcast_to(xr, (8, 128)), jnp.broadcast_to(xi, (8, 128))))
        load(b).wait()
        for it in range(8):
            halves = []
            for half in range(2):
                re = None
                for k, (xr, xi) in enumerate(xs):
                    br = blocks[b, k, 0, pl.ds(16 * it + 8 * half, 8), :]
                    bi = blocks[b, k, 1, pl.ds(16 * it + 8 * half, 8), :]
                    tr = br * xr - bi * xi
                    ti = br * xi + bi * xr
                    re, im = (tr, ti) if re is None else (re + tr, im + ti)
                halves.append((re, im))
            for c in range(2):
                whole = jnp.concatenate([halves[0][c], halves[1][c]], axis=0)
                high = whole.astype(BF16)
                low = (whole - high.astype(F32)).astype(BF16)
                pieces[slot, pl.ds(128 * c + 16 * it, 16), pl.ds(0, 128)] = high
                pieces[slot, pl.ds(128 * c + 16 * it, 16), pl.ds(128, 128)] = low
        return carry

    lax.fori_loop(0, 8, box, 0)
    finish(1, 7)


def final_kernel(got, out_low, out_up):
    sums = [got[k] for k in range(3)]
    for t in range(1, 32):
        for k in range(3):
            sums[k] += got[3 * t + k]
    for p in range(2):
        for c in range(2):
            k = 2 * p + c
            for h in range(2):
                out_low[0, p, pl.ds(c, 1), pl.ds(128 * h, 128)] = sums[p][2 * c + h : 2 * c + h + 1]
            out_up[0, p, pl.ds(c, 1), :] = sums[2][k : k + 1, :96]


def shape(*dims):
    return jax.ShapeDtypeStruct(dims, F32)


def local(
    currents, near_blocks, neighbours, near_count, radiation, interp_leaf, phase_leaf,
    interp_upper, phase_upper, tables_lower, operator_lower, sources_lower, count_lower,
    tables_upper, operator_upper, sources_upper, count_upper,
):
    ints = jnp.int32
    ints = jnp.int32
    kinds = [
        ((16, 256), ints), ((16, 256), ints), ((1, 256), ints), ((7, 32), ints), ((7, 32), ints), ((1, 32), ints),
        ((64, 2, 256), F32), ((64, 2, 96), F32), ((8, 96), F32), ((96, 256), F32),
    ]
    message, *lists = call(
        leaf_kernel, [shape(8, 24, 128)] + [jax.ShapeDtypeStruct(*kind) for kind in kinds], [HBM] * 14,
        [
            pltpu.VMEM((8, 2, 128), F32), pltpu.VMEM((8, 2, 2, 128, 128), F32),
            pltpu.VMEM((128, 256), F32), pltpu.VMEM((8, 256), F32), pltpu.VMEM((32, 128), F32),
            pltpu.VMEM((24, 128), F32), pltpu.SemaphoreType.DMA((37,)), pltpu.SemaphoreType.DMA((10,)),
        ],
        flops=4 << 20, bytes_accessed=3 << 20, first=HBM,
    )(
        currents, radiation, interp_leaf, phase_leaf,
        sources_lower.T, operator_lower.T, count_lower.reshape(1, -1),
        sources_upper.T, operator_upper.T, count_upper.reshape(1, -1),
        tables_lower, tables_upper, phase_upper, interp_upper.T,
    )
    own, message = lax.optimization_barrier((currents, message))
    gathered = lax.all_to_all(message, SAMP, split_axis=0, concat_axis=0, tiled=True)
    size = lax.axis_size(CLUS_SAMP)
    ends = range(7, size - 1, 8)
    cross = lax.ppermute(own, CLUS_SAMP, [(i, i + 1) for i in ends] + [(i + 1, i) for i in ends])

    wa, wb, ua, ub, rot, weights = call(
        prep_kernel,
        [
            shape(32, 8, 8, 128), shape(32, 8, 8, 128), shape(32, 8, 128), shape(32, 8, 128),
            shape(2, 8, 128), jax.ShapeDtypeStruct((96, 768), BF16),
        ],
        [VMEM] * 10,
        [
            pltpu.VMEM((16, 256), ints), pltpu.VMEM((65, 8, 128), F32), pltpu.VMEM((65, 8, 128), F32),
            pltpu.SMEM((16, 256), ints), pltpu.SemaphoreType.DMA,
        ],
        flops=1 << 20, bytes_accessed=4 << 20,
    )(*lists)

    payload = call(
        middle_kernel, shape(96, 4, 128), [VMEM] * 7, [pltpu.VMEM((8, 128), F32)],
        flops=4 << 20, bytes_accessed=3 << 20,
    )(gathered.reshape(192, 128), weights, wa, wb, ua, ub, rot)
    parts = lax.all_to_all(payload, CLUS, split_axis=0, concat_axis=0, tiled=True)

    near_field = call(
        near_kernel, shape(8, 2, 128), [VMEM, VMEM, HBM, HBM, HBM],
        [
            pltpu.VMEM((8, 8, 2, 128, 128), F32),
            pltpu.VMEM((48, 128), F32),
            pltpu.VMEM((2, 256, 256), BF16),
            pltpu.SMEM((8, 8), ints),
            pltpu.SMEM((8,), ints),
            pltpu.SemaphoreType.DMA((10,)),
        ],
        flops=16 << 20, bytes_accessed=8 << 20,
    )(gathered, cross, neighbours, near_count, near_blocks)

    incoming_lower, incoming_upper = call(
        final_kernel, [shape(1, 2, 2, 256), shape(1, 2, 2, 96)], [VMEM],
        flops=1 << 17, bytes_accessed=1 << 18,
    )(parts)
    return near_field, incoming_lower, incoming_upper


def solution(mesh):
    split = Mesh(mesh.devices.reshape(4, 8, 4, 2), CLUS_SAMP)
    whole = P()
    return jax.shard_map(
        local,
        mesh=split,
        in_specs=(
            P(CLUS_SAMP), P(CLUS_SAMP), P(CLUS_SAMP), P(CLUS_SAMP), P(CLUS_SAMP),
            whole, whole, P(None, SAMP), P(None, SAMP),
            whole, whole, whole, whole, P(None, None, SAMP), whole, whole, whole,
        ),
        out_specs=(P(CLUS_SAMP), P(CLUS_SAMP), P(CLUS, None, None, SAMP)),
        check_vma=False,
    )
```

```python
import jax
import jax.numpy as jnp
from jax import lax
from jax.experimental import pallas as pl
from jax.experimental.pallas import tpu as pltpu
from jax.sharding import Mesh
from jax.sharding import PartitionSpec as P

CLUS = ("clus_0", "clus_1")
SAMP = ("samp_0", "samp_1")
CLUS_SAMP = CLUS + SAMP
LAYER = ("clus_0",) + SAMP

F32 = jnp.float32
CHUNKS = 4
BF16 = jnp.bfloat16
VMEM = pl.BlockSpec(memory_space=pltpu.VMEM)
SMEM = pl.BlockSpec(memory_space=pltpu.SMEM)
HBM = pl.BlockSpec(memory_space=pltpu.HBM)


def place():
    return lax.axis_index("clus_0"), lax.axis_index("clus_1"), lax.axis_index("samp_0") * 2 + lax.axis_index("samp_1")


def call(kernel, outs, in_specs, scratch=(), mib=16, flops=0, bytes_accessed=0):
    many = isinstance(outs, (list, tuple))
    run = pl.pallas_call(
        kernel,
        out_shape=outs,
        in_specs=in_specs,
        out_specs=[VMEM] * len(outs) if many else VMEM,
        scratch_shapes=list(scratch),
        compiler_params=pltpu.CompilerParams(vmem_limit_bytes=mib << 20),
        cost_estimate=pl.CostEstimate(flops=flops, bytes_accessed=bytes_accessed, transcendentals=0),
    )

    def placed(*operands):
        return run(
            *(
                x if spec is VMEM else pltpu.with_memory_space_constraint(x, spec.memory_space)
                for x, spec in zip(operands, in_specs)
            )
        )

    return placed


def rows_of(shape, axis):
    return lax.broadcasted_iota(jnp.int32, shape, axis)


def start_all(pairs, sems):
    copies = [pltpu.make_async_copy(a, b, sems.at[i]) for i, (a, b) in enumerate(pairs)]
    for copy in copies:
        copy.start()
    return copies


def pieces_of(x):
    high = x.astype(BF16)
    return high, (x - high.astype(F32)).astype(BF16)


def rotated(cosine, sine, y, p):
    yr = y[16 * p : 16 * p + 8]
    yi = y[16 * p + 8 : 16 * p + 16]
    re = jnp.sum(cosine * yr - sine * yi, axis=0, keepdims=True)
    im = jnp.sum(sine * yr + cosine * yi, axis=0, keepdims=True)
    return re, im


def leaf_kernel(
    cur_h, rad_h, interp_h, phase_h, in0, in1, in2, in3, in4, in5, in6, in7, in8, in9,
    out, to0, to1, to2, to3, to4, to5, to6, to7, to8, to9,
    cur, rad, interp, phase, pat, msg, sems, later_sems,
):
    later_h = [in0, in1, in2, in3, in4, in5, in6, in7, in8, in9]
    later = [to0, to1, to2, to3, to4, to5, to6, to7, to8, to9]
    chunk = 8 // CHUNKS
    spans = [pl.ds(chunk * i, chunk) for i in range(CHUNKS)]
    pairs = [(cur_h, cur)] + [(rad_h.at[span], rad.at[span]) for span in spans]
    copies = start_all(pairs + [(interp_h, interp), (phase_h, phase)], sems)
    others = start_all(list(zip(later_h, later)), later_sems)
    copies[0].wait()
    columns = cur[...].reshape(16, 128).T
    for b in range(8):
        if b % chunk == 0:
            copies[1 + b // chunk].wait()
        cr = jnp.broadcast_to(columns[:, 2 * b : 2 * b + 1], (128, 128))
        ci = jnp.broadcast_to(columns[:, 2 * b + 1 : 2 * b + 2], (128, 128))
        for p in range(2):
            rr = rad[b, p, 0]
            ri = rad[b, p, 1]
            pat[pl.ds(16 * p + b, 1), :] = jnp.sum(rr * cr - ri * ci, axis=0, keepdims=True)
            pat[pl.ds(16 * p + 8 + b, 1), :] = jnp.sum(rr * ci + ri * cr, axis=0, keepdims=True)
    copies[-2].wait()
    copies[-1].wait()
    high, low = pieces_of(interp[...])
    weights_leaf = jnp.concatenate([high, low, high], axis=0)
    cosine = jnp.cos(phase[...])
    sine = jnp.sin(phase[...])
    high, low = pieces_of(pat[...])
    lifted = jnp.dot(
        jnp.concatenate([high, high, low], axis=1), weights_leaf, preferred_element_type=F32
    )
    for p in range(2):
        for c, part in enumerate(rotated(cosine, sine, lifted, p)):
            for h in range(2):
                msg[pl.ds(4 * p + 2 * c + h, 1), :] = part[:, 128 * h : 128 * h + 128]
    whole = msg[...]
    for peer in range(32):
        out[peer] = whole
    for copy in others:
        copy.wait()


def prep_kernel(
    src_low, op_low, cnt_low, src_up, op_up, cnt_up, tab_low, tab_up, phase_up, interp_up,
    wa, wb, ua, ub, rot, weights, code_v, ta, tb, code_s, sem,
):
    y, z, samp = place()
    zero = jnp.zeros((8, 128), F32)
    row = rows_of((8, 128), 0)
    first_half = (row & 1) == 0
    sign_low = jnp.where((row & 2) == 0, -1.0, 1.0).astype(F32)
    sign_up = jnp.where((row & 1) == 0, -1.0, 1.0).astype(F32)[:, :96]
    src = src_low[...]
    used = rows_of(src.shape, 0) < cnt_low[...]
    code = jnp.where(used, 64 - op_low[...], 0)
    for g in range(32):
        box = 64 * (g // 8) + 8 * z + g % 8
        listed = jnp.sum(jnp.where(src == box, code, 0), axis=0, keepdims=True)
        code_v[pl.ds(g, 1), :] = 64 - listed
    code_v[pl.ds(32, 8), :] = jnp.zeros((8, 256), jnp.int32)
    used_up = rows_of(src_up.shape, 0) < cnt_up[...]
    for k in range(4):
        mine = used_up & (src_up[...] == 8 * k + z)
        code_v[pl.ds(32 + k, 1), pl.ds(0, 32)] = jnp.sum(jnp.where(mine, op_up[...] + 1, 0), axis=0, keepdims=True)
    move = pltpu.make_async_copy(code_v, code_s, sem)
    move.start()
    ta[64] = zero
    tb[64] = zero
    rot[0] = zero
    rot[1] = zero
    ua[...] = jnp.zeros((8, 4, 8, 128), F32)
    ub[...] = jnp.zeros((8, 4, 8, 128), F32)

    def expand(n, carry):
        parts = []
        for c in range(2):
            low = jnp.broadcast_to(tab_low[n, pl.ds(c, 1), pl.ds(0, 128)], (8, 128))
            high = jnp.broadcast_to(tab_low[n, pl.ds(c, 1), pl.ds(128, 128)], (8, 128))
            parts.append(jnp.where(first_half, low, high))
        ta[n] = parts[0]
        tb[n] = parts[1] * sign_low
        return carry

    lax.fori_loop(0, 64, expand, 0, unroll=8)
    rot[0, :, pl.ds(0, 96)] = jnp.cos(phase_up[...])
    rot[1, :, pl.ds(0, 96)] = jnp.sin(phase_up[...])
    high, low = pieces_of(interp_up[...])
    weights[...] = jnp.concatenate([high, low, high], axis=1)
    move.wait()

    def target(t, carry):
        clus = 8 * y + t
        for g in range(32):
            n = code_s[g, 8 * clus + samp]
            wa[t, g] = ta[n]
            wb[t, g] = tb[n]
        for k in range(4):
            i = code_s[32 + k, clus]
            n = jnp.maximum(i - 1, 0)
            listed = jnp.where(i > 0, 1.0, 0.0).astype(F32)
            real = jnp.broadcast_to(tab_up[n, pl.ds(0, 1), :], (8, 96)) * listed
            imag = jnp.broadcast_to(tab_up[n, pl.ds(1, 1), :], (8, 96)) * listed
            ua[t, k, :, pl.ds(0, 96)] = real
            ub[t, k, :, pl.ds(0, 96)] = imag * sign_up
        return carry

    lax.fori_loop(0, 8, target, 0)


def middle_kernel(got, weights, wa, wb, ua, ub, rot, out, upper):
    row = rows_of((8, 128), 0)
    halves = []
    for h in range(2):
        parts = [got[pl.ds(64 * y + 2 * k + h, 8, stride=8), :] for y in range(4) for k in range(4)]
        halves.append(jnp.concatenate(parts, axis=0))
    high, low = pieces_of(jnp.concatenate(halves, axis=1))
    lifted = lax.dot_general(
        jnp.concatenate([high, high, low], axis=1), weights[...], (((1,), (1,)), ((), ())),
        preferred_element_type=F32,
    )
    totals = [None] * 8
    for block in range(4):
        plain = [got[pl.ds(64 * block + 8 * o, 8), :] for o in range(8)]
        swapped = [
            jnp.where((row & 2) == 0, pltpu.roll(x, 6, 0), pltpu.roll(x, 2, 0)) for x in plain
        ]
        for t in range(8):
            for o in range(8):
                g = 8 * block + o
                term = wa[t, g] * plain[o] + wb[t, g] * swapped[o]
                totals[t] = term if totals[t] is None else totals[t] + term
    for t in range(8):
        out[3 * t] = totals[t][:4]
        out[3 * t + 1] = totals[t][4:]
    upper[...] = jnp.zeros((4, 8, 128), F32)
    cosine = rot[0][:, :96]
    sine = rot[1][:, :96]
    for y in range(4):
        for p in range(2):
            for c, part in enumerate(rotated(cosine, sine, lifted[32 * y : 32 * y + 32], p)):
                upper[y, pl.ds(2 * p + c, 1), pl.ds(0, 96)] = part
    ups = [upper[y] for y in range(4)]
    pairs = [(up, jnp.where((row & 1) == 0, pltpu.roll(up, 7, 0), pltpu.roll(up, 1, 0))) for up in ups]
    for t in range(8):
        total = None
        for y, (up, up_swapped) in enumerate(pairs):
            term = ua[t, y] * up + ub[t, y] * up_swapped
            total = term if total is None else total + term
        out[3 * t + 2] = total[:4]


def near_kernel(cur_h, even, odd, neighbours_h, count_h, blocks_h, out, cur, blocks, ext, pieces, neighbours, count, sems):
    y, z, samp = place()
    base = (64 * y + 8 * z + samp) * 8 - 8
    lists = start_all([(cur_h, cur), (neighbours_h, neighbours), (count_h, count)], sems.at[pl.ds(8, 3)])

    def load(b):
        return pltpu.make_async_copy(blocks_h.at[b], blocks.at[b], sems.at[b])

    for b in range(8):
        load(b).start()
    parity = samp & 1
    ext[pl.ds(pl.multiple_of(32 * (1 - parity), 8), 16), :] = even[...].reshape(16, 128)
    ext[pl.ds(pl.multiple_of(32 * parity, 8), 16), :] = odd[...].reshape(16, 128)
    pieces[...] = jnp.zeros((2, 256, 256), BF16)
    ones = jnp.ones((16, 256), BF16)
    for one in lists:
        one.wait()
    ext[pl.ds(16, 16), :] = cur[...].reshape(16, 128)

    def finish(slot, b):
        summed = lax.dot_general(
            ones, pieces[slot], (((1,), (1,)), ((), ())), preferred_element_type=F32
        )
        out[b, pl.ds(0, 1), :] = summed[0:1, :128]
        out[b, pl.ds(1, 1), :] = summed[0:1, 128:]

    def box(b, carry):
        slot = b & 1
        finish(1 - slot, jnp.maximum(b - 1, 0))
        xs = []
        for k in range(8):
            i = neighbours[b, k] - base
            keep = jnp.where(k < count[b], 1.0, 0.0).astype(F32)
            xr = ext[pl.ds(2 * i, 1), :] * keep
            xi = ext[pl.ds(2 * i + 1, 1), :] * keep
            xs.append((jnp.broadcast_to(xr, (8, 128)), jnp.broadcast_to(xi, (8, 128))))
        load(b).wait()
        for it in range(8):
            halves = []
            for half in range(2):
                re = None
                for k, (xr, xi) in enumerate(xs):
                    br = blocks[b, k, 0, pl.ds(16 * it + 8 * half, 8), :]
                    bi = blocks[b, k, 1, pl.ds(16 * it + 8 * half, 8), :]
                    tr = br * xr - bi * xi
                    ti = br * xi + bi * xr
                    re, im = (tr, ti) if re is None else (re + tr, im + ti)
                halves.append((re, im))
            for c in range(2):
                whole = jnp.concatenate([halves[0][c], halves[1][c]], axis=0)
                high = whole.astype(BF16)
                low = (whole - high.astype(F32)).astype(BF16)
                pieces[slot, pl.ds(128 * c + 16 * it, 16), pl.ds(0, 128)] = high
                pieces[slot, pl.ds(128 * c + 16 * it, 16), pl.ds(128, 128)] = low
        return carry

    lax.fori_loop(0, 8, box, 0)
    finish(1, 7)


def final_kernel(got, out_low, out_up):
    sums = [got[k] for k in range(3)]
    for t in range(1, 8):
        for k in range(3):
            sums[k] += got[3 * t + k]
    for p in range(2):
        for c in range(2):
            k = 2 * p + c
            for h in range(2):
                out_low[0, p, pl.ds(c, 1), pl.ds(128 * h, 128)] = sums[p][2 * c + h : 2 * c + h + 1]
            out_up[0, p, pl.ds(c, 1), :] = sums[2][k : k + 1, :96]


def shape(*dims):
    return jax.ShapeDtypeStruct(dims, F32)


def local(
    currents, near_blocks, neighbours, near_count, radiation, interp_leaf, phase_leaf,
    interp_upper, phase_upper, tables_lower, operator_lower, sources_lower, count_lower,
    tables_upper, operator_upper, sources_upper, count_upper,
):
    ints = jnp.int32
    ints = jnp.int32
    kinds = [
        ((16, 256), ints), ((16, 256), ints), ((1, 256), ints), ((7, 32), ints), ((7, 32), ints), ((1, 32), ints),
        ((64, 2, 256), F32), ((64, 2, 96), F32), ((8, 96), F32), ((96, 256), F32),
    ]
    message, *lists = call(
        leaf_kernel, [shape(32, 8, 128)] + [jax.ShapeDtypeStruct(*kind) for kind in kinds], [HBM] * 14,
        [
            pltpu.VMEM((8, 2, 128), F32), pltpu.VMEM((8, 2, 2, 128, 128), F32),
            pltpu.VMEM((128, 256), F32), pltpu.VMEM((8, 256), F32), pltpu.VMEM((32, 128), F32),
            pltpu.VMEM((8, 128), F32), pltpu.SemaphoreType.DMA((7,)), pltpu.SemaphoreType.DMA((10,)),
        ],
        flops=4 << 20, bytes_accessed=3 << 20,
    )(
        currents, radiation, interp_leaf, phase_leaf,
        sources_lower.T, operator_lower.T, count_lower.reshape(1, -1),
        sources_upper.T, operator_upper.T, count_upper.reshape(1, -1),
        tables_lower, tables_upper, phase_upper, interp_upper.T,
    )
    own, message = lax.optimization_barrier((currents, message))
    gathered = lax.all_to_all(message, LAYER, split_axis=0, concat_axis=0, tiled=True)
    size = lax.axis_size(CLUS_SAMP)
    even = lax.ppermute(own, CLUS_SAMP, [(i, i ^ 1) for i in range(size)])
    odd = lax.ppermute(own, CLUS_SAMP, [(i, ((i + 1) ^ 1) - 1) for i in range(1, size - 1)])

    wa, wb, ua, ub, rot, weights = call(
        prep_kernel,
        [
            shape(8, 32, 8, 128), shape(8, 32, 8, 128), shape(8, 4, 8, 128), shape(8, 4, 8, 128),
            shape(2, 8, 128), jax.ShapeDtypeStruct((96, 768), BF16),
        ],
        [VMEM] * 10,
        [
            pltpu.VMEM((40, 256), ints), pltpu.VMEM((65, 8, 128), F32), pltpu.VMEM((65, 8, 128), F32),
            pltpu.SMEM((40, 256), ints), pltpu.SemaphoreType.DMA,
        ],
        flops=1 << 20, bytes_accessed=4 << 20,
    )(*lists)

    payload = call(
        middle_kernel, shape(24, 4, 128), [VMEM] * 7, [pltpu.VMEM((4, 8, 128), F32)],
        flops=4 << 20, bytes_accessed=3 << 20,
    )(gathered.reshape(256, 128), weights, wa, wb, ua, ub, rot)
    parts = lax.all_to_all(payload, "clus_1", split_axis=0, concat_axis=0, tiled=True)

    near_field = call(
        near_kernel, shape(8, 2, 128), [HBM, VMEM, VMEM, HBM, HBM, HBM],
        [
            pltpu.VMEM((8, 2, 128), F32),
            pltpu.VMEM((8, 8, 2, 128, 128), F32),
            pltpu.VMEM((48, 128), F32),
            pltpu.VMEM((2, 256, 256), BF16),
            pltpu.SMEM((8, 8), ints),
            pltpu.SMEM((8,), ints),
            pltpu.SemaphoreType.DMA((11,)),
        ],
        flops=16 << 20, bytes_accessed=8 << 20,
    )(currents, even, odd, neighbours, near_count, near_blocks)

    incoming_lower, incoming_upper = call(
        final_kernel, [shape(1, 2, 2, 256), shape(1, 2, 2, 96)], [VMEM],
        flops=1 << 17, bytes_accessed=1 << 18,
    )(parts)
    return near_field, incoming_lower, incoming_upper


def solution(mesh):
    split = Mesh(mesh.devices.reshape(4, 8, 4, 2), CLUS_SAMP)
    whole = P()
    return jax.shard_map(
        local,
        mesh=split,
        in_specs=(
            P(CLUS_SAMP), P(CLUS_SAMP), P(CLUS_SAMP), P(CLUS_SAMP), P(CLUS_SAMP),
            whole, whole, P(None, SAMP), P(None, SAMP),
            whole, whole, whole, whole, P(None, None, SAMP), whole, whole, whole,
        ),
        out_specs=(P(CLUS_SAMP), P(CLUS_SAMP), P(CLUS, None, None, SAMP)),
        check_vma=False,
    )
```

```python
import jax
import jax.numpy as jnp
from jax import lax
from jax.experimental import pallas as pl
from jax.experimental.pallas import tpu as pltpu
from jax.sharding import Mesh
from jax.sharding import PartitionSpec as P

CLUS = ("clus_0", "clus_1")
SAMP = ("samp_0", "samp_1")
CLUS_SAMP = CLUS + SAMP
LAYER = ("clus_0",) + SAMP

F32 = jnp.float32
CHUNKS = 4
BF16 = jnp.bfloat16
VMEM = pl.BlockSpec(memory_space=pltpu.VMEM)
SMEM = pl.BlockSpec(memory_space=pltpu.SMEM)
HBM = pl.BlockSpec(memory_space=pltpu.HBM)


def place():
    return lax.axis_index("clus_0"), lax.axis_index("clus_1"), lax.axis_index("samp_0") * 2 + lax.axis_index("samp_1")


def call(kernel, outs, in_specs, scratch=(), mib=16, flops=0, bytes_accessed=0):
    many = isinstance(outs, (list, tuple))
    run = pl.pallas_call(
        kernel,
        out_shape=outs,
        in_specs=in_specs,
        out_specs=[VMEM] * len(outs) if many else VMEM,
        scratch_shapes=list(scratch),
        compiler_params=pltpu.CompilerParams(vmem_limit_bytes=mib << 20),
        cost_estimate=pl.CostEstimate(flops=flops, bytes_accessed=bytes_accessed, transcendentals=0),
    )

    def placed(*operands):
        return run(
            *(
                x if spec is VMEM else pltpu.with_memory_space_constraint(x, spec.memory_space)
                for x, spec in zip(operands, in_specs)
            )
        )

    return placed


def rows_of(shape, axis):
    return lax.broadcasted_iota(jnp.int32, shape, axis)


def start_all(pairs, sems):
    copies = [pltpu.make_async_copy(a, b, sems.at[i]) for i, (a, b) in enumerate(pairs)]
    for copy in copies:
        copy.start()
    return copies


def pieces_of(x):
    high = x.astype(BF16)
    return high, (x - high.astype(F32)).astype(BF16)


def rotated(cosine, sine, y, p):
    yr = y[16 * p : 16 * p + 8]
    yi = y[16 * p + 8 : 16 * p + 16]
    re = jnp.sum(cosine * yr - sine * yi, axis=0, keepdims=True)
    im = jnp.sum(sine * yr + cosine * yi, axis=0, keepdims=True)
    return re, im


def leaf_kernel(
    cur_h, rad_h, interp_h, phase_h, in0, in1, in2, in3, in4, in5,
    out, to0, to1, to2, to3, to4, to5,
    cur, rad, interp, phase, pat, msg, sems, later_sems,
):
    later_h = [in0, in1, in2, in3, in4, in5]
    later = [to0, to1, to2, to3, to4, to5]
    chunk = 8 // CHUNKS
    spans = [pl.ds(chunk * i, chunk) for i in range(CHUNKS)]
    pairs = [(cur_h, cur)] + [(rad_h.at[span], rad.at[span]) for span in spans]
    copies = start_all(pairs + [(interp_h, interp), (phase_h, phase)], sems)
    others = start_all(list(zip(later_h, later)), later_sems)
    copies[0].wait()
    columns = cur[...].reshape(16, 128).T
    for b in range(8):
        if b % chunk == 0:
            copies[1 + b // chunk].wait()
        cr = jnp.broadcast_to(columns[:, 2 * b : 2 * b + 1], (128, 128))
        ci = jnp.broadcast_to(columns[:, 2 * b + 1 : 2 * b + 2], (128, 128))
        for p in range(2):
            rr = rad[b, p, 0]
            ri = rad[b, p, 1]
            pat[pl.ds(16 * p + b, 1), :] = jnp.sum(rr * cr - ri * ci, axis=0, keepdims=True)
            pat[pl.ds(16 * p + 8 + b, 1), :] = jnp.sum(rr * ci + ri * cr, axis=0, keepdims=True)
    copies[-2].wait()
    copies[-1].wait()
    high, low = pieces_of(interp[...])
    weights_leaf = jnp.concatenate([high, low, high], axis=0)
    cosine = jnp.cos(phase[...])
    sine = jnp.sin(phase[...])
    high, low = pieces_of(pat[...])
    lifted = jnp.dot(
        jnp.concatenate([high, high, low], axis=1), weights_leaf, preferred_element_type=F32
    )
    for p in range(2):
        for c, part in enumerate(rotated(cosine, sine, lifted, p)):
            for h in range(2):
                msg[pl.ds(4 * p + 2 * c + h, 1), :] = part[:, 128 * h : 128 * h + 128]
    whole = msg[...]
    for peer in range(32):
        out[peer] = whole
    for copy in others:
        copy.wait()


def prep_kernel(
    src_low, op_low, cnt_low, src_up, op_up, cnt_up, tab_low_h, tab_up_h, phase_up_h, interp_up_h,
    wa, wb, ua, ub, rot, weights, tab_low, tab_up, phase_up, interp_up, code_v, ta, tb, code_s, sem, sems,
):
    copies = start_all(
        [(tab_low_h, tab_low), (tab_up_h, tab_up), (phase_up_h, phase_up), (interp_up_h, interp_up)], sems
    )
    y, z, samp = place()
    zero = jnp.zeros((8, 128), F32)
    row = rows_of((8, 128), 0)
    first_half = (row & 1) == 0
    sign_low = jnp.where((row & 2) == 0, -1.0, 1.0).astype(F32)
    sign_up = jnp.where((row & 1) == 0, -1.0, 1.0).astype(F32)[:, :96]
    src = src_low[...]
    used = rows_of(src.shape, 0) < cnt_low[...]
    code = jnp.where(used, 64 - op_low[...], 0)
    for g in range(32):
        box = 64 * (g // 8) + 8 * z + g % 8
        listed = jnp.sum(jnp.where(src == box, code, 0), axis=0, keepdims=True)
        code_v[pl.ds(g, 1), :] = 64 - listed
    code_v[pl.ds(32, 8), :] = jnp.zeros((8, 256), jnp.int32)
    used_up = rows_of(src_up.shape, 0) < cnt_up[...]
    for k in range(4):
        mine = used_up & (src_up[...] == 8 * k + z)
        code_v[pl.ds(32 + k, 1), pl.ds(0, 32)] = jnp.sum(jnp.where(mine, op_up[...] + 1, 0), axis=0, keepdims=True)
    move = pltpu.make_async_copy(code_v, code_s, sem)
    move.start()
    ta[64] = zero
    tb[64] = zero
    rot[0] = zero
    rot[1] = zero
    ua[...] = jnp.zeros((8, 4, 8, 128), F32)
    ub[...] = jnp.zeros((8, 4, 8, 128), F32)

    for copy in copies:
        copy.wait()

    def expand(n, carry):
        parts = []
        for c in range(2):
            low = jnp.broadcast_to(tab_low[n, pl.ds(c, 1), pl.ds(0, 128)], (8, 128))
            high = jnp.broadcast_to(tab_low[n, pl.ds(c, 1), pl.ds(128, 128)], (8, 128))
            parts.append(jnp.where(first_half, low, high))
        ta[n] = parts[0]
        tb[n] = parts[1] * sign_low
        return carry

    lax.fori_loop(0, 64, expand, 0, unroll=8)
    rot[0, :, pl.ds(0, 96)] = jnp.cos(phase_up[...])
    rot[1, :, pl.ds(0, 96)] = jnp.sin(phase_up[...])
    high, low = pieces_of(interp_up[...])
    weights[...] = jnp.concatenate([high, low, high], axis=1)
    move.wait()

    def target(t, carry):
        clus = 8 * y + t
        for g in range(32):
            n = code_s[g, 8 * clus + samp]
            wa[t, g] = ta[n]
            wb[t, g] = tb[n]
        for k in range(4):
            i = code_s[32 + k, clus]
            n = jnp.maximum(i - 1, 0)
            listed = jnp.where(i > 0, 1.0, 0.0).astype(F32)
            real = jnp.broadcast_to(tab_up[n, pl.ds(0, 1), :], (8, 96)) * listed
            imag = jnp.broadcast_to(tab_up[n, pl.ds(1, 1), :], (8, 96)) * listed
            ua[t, k, :, pl.ds(0, 96)] = real
            ub[t, k, :, pl.ds(0, 96)] = imag * sign_up
        return carry

    lax.fori_loop(0, 8, target, 0)


def middle_kernel(got, weights, wa, wb, ua, ub, rot, out, upper):
    row = rows_of((8, 128), 0)
    halves = []
    for h in range(2):
        parts = [got[pl.ds(64 * y + 2 * k + h, 8, stride=8), :] for y in range(4) for k in range(4)]
        halves.append(jnp.concatenate(parts, axis=0))
    high, low = pieces_of(jnp.concatenate(halves, axis=1))
    lifted = lax.dot_general(
        jnp.concatenate([high, high, low], axis=1), weights[...], (((1,), (1,)), ((), ())),
        preferred_element_type=F32,
    )
    totals = [None] * 8
    for block in range(4):
        plain = [got[pl.ds(64 * block + 8 * o, 8), :] for o in range(8)]
        swapped = [
            jnp.where((row & 2) == 0, pltpu.roll(x, 6, 0), pltpu.roll(x, 2, 0)) for x in plain
        ]
        for t in range(8):
            for o in range(8):
                g = 8 * block + o
                term = wa[t, g] * plain[o] + wb[t, g] * swapped[o]
                totals[t] = term if totals[t] is None else totals[t] + term
    for t in range(8):
        out[3 * t] = totals[t][:4]
        out[3 * t + 1] = totals[t][4:]
    upper[...] = jnp.zeros((4, 8, 128), F32)
    cosine = rot[0][:, :96]
    sine = rot[1][:, :96]
    for y in range(4):
        for p in range(2):
            for c, part in enumerate(rotated(cosine, sine, lifted[32 * y : 32 * y + 32], p)):
                upper[y, pl.ds(2 * p + c, 1), pl.ds(0, 96)] = part
    ups = [upper[y] for y in range(4)]
    pairs = [(up, jnp.where((row & 1) == 0, pltpu.roll(up, 7, 0), pltpu.roll(up, 1, 0))) for up in ups]
    for t in range(8):
        total = None
        for y, (up, up_swapped) in enumerate(pairs):
            term = ua[t, y] * up + ub[t, y] * up_swapped
            total = term if total is None else total + term
        out[3 * t + 2] = total[:4]


def near_kernel(cur_h, even, odd, neighbours_h, count_h, blocks_h, out, cur, blocks, ext, pieces, neighbours, count, sems):
    y, z, samp = place()
    base = (64 * y + 8 * z + samp) * 8 - 8
    lists = start_all([(cur_h, cur), (neighbours_h, neighbours), (count_h, count)], sems.at[pl.ds(8, 3)])

    def load(b):
        return pltpu.make_async_copy(blocks_h.at[b], blocks.at[b], sems.at[b])

    for b in range(8):
        load(b).start()
    parity = samp & 1
    ext[pl.ds(pl.multiple_of(32 * (1 - parity), 8), 16), :] = even[...].reshape(16, 128)
    ext[pl.ds(pl.multiple_of(32 * parity, 8), 16), :] = odd[...].reshape(16, 128)
    pieces[...] = jnp.zeros((2, 256, 256), BF16)
    ones = jnp.ones((16, 256), BF16)
    for one in lists:
        one.wait()
    ext[pl.ds(16, 16), :] = cur[...].reshape(16, 128)

    def finish(slot, b):
        summed = lax.dot_general(
            ones, pieces[slot], (((1,), (1,)), ((), ())), preferred_element_type=F32
        )
        out[b, pl.ds(0, 1), :] = summed[0:1, :128]
        out[b, pl.ds(1, 1), :] = summed[0:1, 128:]

    def box(b, carry):
        slot = b & 1
        finish(1 - slot, jnp.maximum(b - 1, 0))
        xs = []
        for k in range(8):
            i = neighbours[b, k] - base
            keep = jnp.where(k < count[b], 1.0, 0.0).astype(F32)
            xr = ext[pl.ds(2 * i, 1), :] * keep
            xi = ext[pl.ds(2 * i + 1, 1), :] * keep
            xs.append((jnp.broadcast_to(xr, (8, 128)), jnp.broadcast_to(xi, (8, 128))))
        load(b).wait()
        for it in range(8):
            halves = []
            for half in range(2):
                re = None
                for k, (xr, xi) in enumerate(xs):
                    br = blocks[b, k, 0, pl.ds(16 * it + 8 * half, 8), :]
                    bi = blocks[b, k, 1, pl.ds(16 * it + 8 * half, 8), :]
                    tr = br * xr - bi * xi
                    ti = br * xi + bi * xr
                    re, im = (tr, ti) if re is None else (re + tr, im + ti)
                halves.append((re, im))
            for c in range(2):
                whole = jnp.concatenate([halves[0][c], halves[1][c]], axis=0)
                high = whole.astype(BF16)
                low = (whole - high.astype(F32)).astype(BF16)
                pieces[slot, pl.ds(128 * c + 16 * it, 16), pl.ds(0, 128)] = high
                pieces[slot, pl.ds(128 * c + 16 * it, 16), pl.ds(128, 128)] = low
        return carry

    lax.fori_loop(0, 8, box, 0)
    finish(1, 7)


def final_kernel(got, out_low, out_up):
    sums = [got[k] for k in range(3)]
    for t in range(1, 8):
        for k in range(3):
            sums[k] += got[3 * t + k]
    for p in range(2):
        for c in range(2):
            k = 2 * p + c
            for h in range(2):
                out_low[0, p, pl.ds(c, 1), pl.ds(128 * h, 128)] = sums[p][2 * c + h : 2 * c + h + 1]
            out_up[0, p, pl.ds(c, 1), :] = sums[2][k : k + 1, :96]


def shape(*dims):
    return jax.ShapeDtypeStruct(dims, F32)


def local(
    currents, near_blocks, neighbours, near_count, radiation, interp_leaf, phase_leaf,
    interp_upper, phase_upper, tables_lower, operator_lower, sources_lower, count_lower,
    tables_upper, operator_upper, sources_upper, count_upper,
):
    ints = jnp.int32
    ints = jnp.int32
    kinds = [
        ((16, 256), ints), ((16, 256), ints), ((1, 256), ints), ((7, 32), ints), ((7, 32), ints), ((1, 32), ints),
    ]
    message, *lists = call(
        leaf_kernel, [shape(32, 8, 128)] + [jax.ShapeDtypeStruct(*kind) for kind in kinds], [HBM] * 10,
        [
            pltpu.VMEM((8, 2, 128), F32), pltpu.VMEM((8, 2, 2, 128, 128), F32),
            pltpu.VMEM((128, 256), F32), pltpu.VMEM((8, 256), F32), pltpu.VMEM((32, 128), F32),
            pltpu.VMEM((8, 128), F32), pltpu.SemaphoreType.DMA((7,)), pltpu.SemaphoreType.DMA((6,)),
        ],
        flops=4 << 20, bytes_accessed=3 << 20,
    )(
        currents, radiation, interp_leaf, phase_leaf,
        sources_lower.T, operator_lower.T, count_lower.reshape(1, -1),
        sources_upper.T, operator_upper.T, count_upper.reshape(1, -1),
    )
    own, message = lax.optimization_barrier((currents, message))
    gathered = lax.all_to_all(message, LAYER, split_axis=0, concat_axis=0, tiled=True)
    size = lax.axis_size(CLUS_SAMP)
    even = lax.ppermute(own, CLUS_SAMP, [(i, i ^ 1) for i in range(size)])
    odd = lax.ppermute(own, CLUS_SAMP, [(i, ((i + 1) ^ 1) - 1) for i in range(1, size - 1)])

    wa, wb, ua, ub, rot, weights = call(
        prep_kernel,
        [
            shape(8, 32, 8, 128), shape(8, 32, 8, 128), shape(8, 4, 8, 128), shape(8, 4, 8, 128),
            shape(2, 8, 128), jax.ShapeDtypeStruct((96, 768), BF16),
        ],
        [VMEM] * 6 + [HBM] * 4,
        [
            pltpu.VMEM((64, 2, 256), F32), pltpu.VMEM((64, 2, 96), F32), pltpu.VMEM((8, 96), F32),
            pltpu.VMEM((96, 256), F32), pltpu.VMEM((40, 256), ints), pltpu.VMEM((65, 8, 128), F32), pltpu.VMEM((65, 8, 128), F32),
            pltpu.SMEM((40, 256), ints), pltpu.SemaphoreType.DMA, pltpu.SemaphoreType.DMA((4,)),
        ],
        flops=1 << 20, bytes_accessed=4 << 20,
    )(*lists, tables_lower, tables_upper, phase_upper, interp_upper.T)

    payload = call(
        middle_kernel, shape(24, 4, 128), [VMEM] * 7, [pltpu.VMEM((4, 8, 128), F32)],
        flops=4 << 20, bytes_accessed=3 << 20,
    )(gathered.reshape(256, 128), weights, wa, wb, ua, ub, rot)
    parts = lax.all_to_all(payload, "clus_1", split_axis=0, concat_axis=0, tiled=True)

    near_field = call(
        near_kernel, shape(8, 2, 128), [HBM, VMEM, VMEM, HBM, HBM, HBM],
        [
            pltpu.VMEM((8, 2, 128), F32),
            pltpu.VMEM((8, 8, 2, 128, 128), F32),
            pltpu.VMEM((48, 128), F32),
            pltpu.VMEM((2, 256, 256), BF16),
            pltpu.SMEM((8, 8), ints),
            pltpu.SMEM((8,), ints),
            pltpu.SemaphoreType.DMA((11,)),
        ],
        flops=16 << 20, bytes_accessed=8 << 20,
    )(currents, even, odd, neighbours, near_count, near_blocks)

    incoming_lower, incoming_upper = call(
        final_kernel, [shape(1, 2, 2, 256), shape(1, 2, 2, 96)], [VMEM],
        flops=1 << 17, bytes_accessed=1 << 18,
    )(parts)
    return near_field, incoming_lower, incoming_upper


def solution(mesh):
    split = Mesh(mesh.devices.reshape(4, 8, 4, 2), CLUS_SAMP)
    whole = P()
    return jax.shard_map(
        local,
        mesh=split,
        in_specs=(
            P(CLUS_SAMP), P(CLUS_SAMP), P(CLUS_SAMP), P(CLUS_SAMP), P(CLUS_SAMP),
            whole, whole, P(None, SAMP), P(None, SAMP),
            whole, whole, whole, whole, P(None, None, SAMP), whole, whole, whole,
        ),
        out_specs=(P(CLUS_SAMP), P(CLUS_SAMP), P(CLUS, None, None, SAMP)),
        check_vma=False,
    )
```
